32 devices in a mesh: blk: 8 (over z, y), layer: 4 (over x, core).
Axes of the slice: x: 2, y: 2, z: 4, core: 2. Of those that a mesh axis runs over, the one named last changes fastest.
Arguments:
- source: float32 [64, 512, 128], P('layer', 'blk'), may hold values from -18 to 18
- sigma_ref: float32 [64, 512, 128], P('layer', 'blk'), may hold values from 0.3 to 3
- owner: int32 [64, 512], P('layer', 'blk'), may hold values from 0 to 31, as said below
- slot: int32 [64, 512], P('layer', 'blk'), may hold values from 0 to 1023, as said below
- temp_old: float32 [32768, 128], P(('blk', 'layer')), may hold values from 0 to 2
- heat_cap: float32 [32768, 128], P(('blk', 'layer')), may hold values from 0.5 to 4
- conduct: float32 [32768, 128], P(('blk', 'layer')), may hold values from 0.2 to 2
Outputs:
- potential: float32 [64, 512, 128], P('layer', 'blk')
- temp_new: float32 [32768, 128], P(('blk', 'layer'))
The draws below stay inside these ranges and needn't reach their ends.
Inputs may be any that keep to these rules, and one draw needn't show every extreme that they name: Among the 1024 blocks of one electric subdomain, at most 64 name the same owner, and 64 is reached in every subdomain. The pairs (owner, slot) are all different: every owner receives exactly 1024 blocks, one for each of its rows.
All inputs are finite; a program needn't handle non-finite values.
Results may differ from the reference program's by a relative error of at most 0.00002.
Values sent between devices are 32-bit elements; how exact they have to be, the bound alone decides.
A program may use at most 64 MiB of HBM per device.

```python
import math
import jax
import jax.numpy as jnp

CA = 16
CR = 64
RAD = 128
SWEEPS = 3
JACOBI = 2
SECTORS = 8
SLABS = 4
DOMAINS = 32
NBLK = 1024
BLOCKS_EACH = 32
NA = 64
NRG = 512
THERMAL_ROWS = 32768


def intersection_maps(key):
    base_key = jax.random.fold_in(key, 7)
    key_pattern, key_receive, key_send = jax.random.split(base_key, 3)
    quarter = DOMAINS // 4
    pattern = jnp.concatenate([jnp.full((quarter,), 2 * BLOCKS_EACH, jnp.int32), jnp.full((DOMAINS - 2 * quarter,), BLOCKS_EACH, jnp.int32), jnp.zeros((quarter,), jnp.int32)])
    shuffle = jax.random.permutation(key_pattern, DOMAINS).astype(jnp.int32)
    source_ids = jnp.arange(DOMAINS, dtype=jnp.int32)
    counts = pattern[(shuffle[None, :] + source_ids[:, None]) % DOMAINS]
    ends = jnp.cumsum(counts, axis=1)
    places = jnp.arange(NBLK, dtype=jnp.int32)
    target = jax.vmap(lambda row_ends: jnp.searchsorted(row_ends, places, side='right'))(ends).astype(jnp.int32)
    begins = jnp.take_along_axis(ends - counts, target, axis=1)
    within = places[None, :] - begins
    offsets = jnp.cumsum(counts, axis=0) - counts
    base_slot = offsets[source_ids[:, None], target] + within
    receive_perm = jax.vmap(lambda sub_key: jax.random.permutation(sub_key, NBLK))(jax.random.split(key_receive, DOMAINS)).astype(jnp.int32)
    slot_table = receive_perm[target, base_slot]
    send_perm = jax.vmap(lambda sub_key: jax.random.permutation(sub_key, NBLK))(jax.random.split(key_send, DOMAINS)).astype(jnp.int32)
    owner_rows = jnp.take_along_axis(target, send_perm, axis=1)
    slot_rows = jnp.take_along_axis(slot_table, send_perm, axis=1)

    def arrange(values):
        return values.reshape(SECTORS, SLABS, CA, CR).transpose(1, 2, 0, 3).reshape(NA, NRG).astype(jnp.int32)
    return (arrange(owner_rows), arrange(slot_rows))


def draw_owner(key, part):
    return intersection_maps(key)[0]


def draw_slot(key, part):
    return intersection_maps(key)[1]


def draw_source(key, part):
    cycle_pos = jnp.arange(NRG, dtype=jnp.float32) / NRG
    amplitude = 1.0 + 2.0 * cycle_pos
    values = jnp.clip(jax.random.normal(key, (NA, NRG, RAD), jnp.float32), -6.0, 6.0)
    return (values * amplitude[None, :, None]).astype(jnp.float32)


def shard_levels(own_key, dims, pieces, low, high):
    def one(position, shards_of):
        steps = jax.random.uniform(jax.random.fold_in(jax.random.fold_in(own_key, 6), position), (shards_of,), jnp.float32, low / len(pieces), high / len(pieces))
        return jnp.repeat(jnp.exp(steps), dims[position] // shards_of).reshape((-1,) + (1,) * (len(dims) - position - 1))

    level = one(*pieces[0])
    for cut in pieces[1:]:
        level = level * one(*cut)
    return level


def setup_inputs(seed: int = 0) -> dict:
    key_of = jax.random.split(jax.random.key(seed), 8)
    return {
        "source": draw_source(jax.random.fold_in(key_of[7], 71), 0),
        "sigma_ref": jnp.clip(jnp.exp(math.log(3.0) - 2.3025851 * jax.random.uniform(key_of[1], (NA, NRG, RAD), jnp.float32) ** shard_levels(key_of[1], (NA, NRG, RAD), ((0, 4), (1, 8)), -0.2, 0.2)), 0.3, 3.0),
        "owner": draw_owner(jax.random.fold_in(key_of[7], 71), 0),
        "slot": draw_slot(jax.random.fold_in(key_of[7], 71), 0),
        "temp_old": jnp.clip(2.0 * jax.random.uniform(key_of[4], (THERMAL_ROWS, RAD), jnp.float32) ** shard_levels(key_of[4], (THERMAL_ROWS, RAD), ((0, 32),), -0.2, 0.2), 0.0, 2.0),
        "heat_cap": jnp.clip(jnp.exp(math.log(4.0) - 2.0794415 * jax.random.uniform(key_of[5], (THERMAL_ROWS, RAD), jnp.float32) ** shard_levels(key_of[5], (THERMAL_ROWS, RAD), ((0, 32),), -0.2, 0.2)), 0.5, 4.0),
        "conduct": jnp.clip(jnp.exp(math.log(2.0) - 2.3025851 * jax.random.uniform(key_of[6], (THERMAL_ROWS, RAD), jnp.float32) ** shard_levels(key_of[6], (THERMAL_ROWS, RAD), ((0, 32),), -0.2, 0.2)), 0.2, 2.0),
    }


COUPLE = 0.4
THETA = 1.125
DELTA = 0.875


def neighbours(field):
    axial = jnp.pad(field, ((1, 1), (0, 0), (0, 0)))
    radial = jnp.pad(field, ((0, 0), (0, 0), (1, 1)))
    return [axial[2:], axial[:-2], jnp.roll(field, -1, 1), jnp.roll(field, 1, 1), radial[:, :, 2:], radial[:, :, :-2]]


def electric(source, cond_here):
    couplings = [0.5 * (cond_here + other) for other in neighbours(cond_here)]
    diag_sum = couplings[0]
    for coupling in couplings[1:]:
        diag_sum = diag_sum + coupling
    inv_diag = 1.0 / diag_sum

    def operate(field):
        result = jnp.zeros_like(field)
        for coupling, other in zip(couplings, neighbours(field)):
            result = result + coupling * (field - other)
        return result

    ratio = THETA / DELTA
    potential = jnp.zeros_like(source)
    residual = source
    search_dir = inv_diag * residual / THETA
    rho_now = 1.0 / ratio
    for sweep in range(SWEEPS):
        potential = potential + search_dir
        if sweep + 1 < SWEEPS:
            residual = residual - operate(search_dir)
            rho_next = 1.0 / (2.0 * ratio - rho_now)
            search_dir = (rho_next * rho_now) * search_dir + (2.0 * rho_next / DELTA) * (inv_diag * residual)
            rho_now = rho_next
    return potential


def joule(potential, cond_here):
    result = jnp.zeros_like(potential)
    for other in neighbours(potential):
        gap = potential - other
        result = result + 0.5 * gap * gap
    return cond_here * result


def thermal_step(temp_old, heat_cap, conduct, heat):
    faces = 0.5 * (conduct[:, 1:] + conduct[:, :-1])
    edge = jnp.zeros((conduct.shape[0], 1), jnp.float32)
    left_cond = jnp.concatenate([edge, faces], axis=1)
    right_cond = jnp.concatenate([faces, edge], axis=1)
    diag_sum = heat_cap + left_cond + right_cond
    target = heat_cap * temp_old + heat
    current = temp_old
    for sweep in range(JACOBI):
        before = jnp.concatenate([edge, current[:, :-1]], axis=1)
        after = jnp.concatenate([current[:, 1:], edge], axis=1)
        current = (target + left_cond * before + right_cond * after) / diag_sum
    return current


def reference(source, sigma_ref, owner, slot, temp_old, heat_cap, conduct):
    rows_index = (owner * NBLK + slot).reshape(-1).astype(jnp.int32)
    temp_here = jnp.take(temp_old, rows_index, axis=0).reshape(NA, NRG, RAD)
    cond_here = sigma_ref / (1.0 + COUPLE * temp_here)
    potential = electric(source, cond_here)
    power = joule(potential, cond_here)
    total = jnp.sum(power)
    scaled = power * ((NA * NRG * RAD) / total)
    heat = jnp.zeros((THERMAL_ROWS, RAD), jnp.float32).at[rows_index].set(scaled.reshape(-1, RAD))
    temp_new = thermal_step(temp_old, heat_cap, conduct, heat)
    return (potential, temp_new)
```

```python
import jax
import jax.numpy as jnp
from jax import lax
from jax.experimental import pallas as pl
from jax.experimental.pallas import tpu as pltpu
from jax.sharding import PartitionSpec as P

JACOBI = 2
COUPLE = 0.4
THETA = 1.125
DELTA = 0.875

WIDE = 4
ROWS = 8
EDGE = 4
LANES = 128
MESH = pl.DeviceIdType.MESH
DIRECTIONS = [(a, r) for r in (-1, 1, 0) for a in (-1, 1, 0) if (a, r) != (0, 0)]


def iota(shape, axis):
    return lax.broadcasted_iota(jnp.int32, shape, axis)


def ones(mask):
    return jnp.where(mask, 1.0, 0.0)


def dot(x, y, over):
    return lax.dot_general(
        x.astype(jnp.bfloat16), y.astype(jnp.bfloat16), (over, ((), ())),
        preferred_element_type=jnp.float32,
    )


def route(owner, slot, ask, places, blocks, cap):
    ca, cr = owner.shape
    n = ask.shape[0]
    earlier = ones(iota((cr, cr), 0) < iota((cr, cr), 1))
    seen = jnp.zeros((n, 1), jnp.float32)
    table = jnp.zeros((4 * n, LANES), jnp.float32)
    lane = iota((n, cr), 1).astype(jnp.float32)
    places[...] = jnp.zeros(places.shape, jnp.int32)
    for a in range(ca):
        name = owner[a : a + 1, :]
        mine = ones(iota((n, cr), 0) == name)
        before = dot(mine, earlier, ((1,), (0,))) + seen
        within = jnp.sum(mine * before, axis=0, keepdims=True).astype(jnp.int32)
        seen = seen + jnp.sum(mine, axis=1, keepdims=True)
        places[a, :, 0:cr] = jnp.clip(name * cap + within, 0, n * cap - 1)
        here = ones(iota((LANES, cr), 0) == within)
        code = slot[a : a + 1, :] + 1
        high = (code >> 5).astype(jnp.float32)
        low = (code & 31).astype(jnp.float32)
        digits = jnp.concatenate([mine * high, mine * low, mine * float(a), mine * lane], axis=0)
        table = table + dot(digits, here, ((1,), (1,)))
    codes = (table[0:n] * 32.0 + table[n : 2 * n]).astype(jnp.int32)
    block = (table[2 * n : 3 * n] * float(cr) + table[3 * n :]).astype(jnp.int32)
    for j in range(n):
        ask[j] = codes[j : j + 1]
        blocks[j] = jnp.clip(block[j : j + 1], 0, ca * cr - 1)


def invert(wanted, where_from, stride):
    n = wanted.shape[0]
    hn = where_from.shape[0]
    ln = 32

    def body(j, table):
        code = wanted[j] - 1
        at = ones(iota((hn, LANES), 0) == (code >> 5))
        low = ones(iota((ln, LANES), 0) == (code & 31))
        lane = iota((hn, LANES), 1).astype(jnp.float32)
        digits = jnp.concatenate([at * j.astype(jnp.float32), at * lane], axis=0)
        return table + dot(digits, low, ((1,), (1,)))

    table = lax.fori_loop(0, n, body, jnp.zeros((2 * hn, ln), jnp.float32), unroll=4)
    found = (table[:hn] * float(stride) + table[hn:]).astype(jnp.int32)
    found = jnp.clip(found, 0, n * stride - 1)
    where_from[...] = jnp.zeros(where_from.shape, jnp.int32)
    for h in range(hn):
        where_from[h, :, 0:ln] = found[h : h + 1]


def exchange_kernel(
    layers, blks,
    source, sigma_in, owner_in, slot_in, old_in, cap_in, conduct_in,
    potential, heat, sums, inv_d, base, first_t, left_n, right_n,
    arrived, where_v, where_from,
    owner, slot, sigma, temp_old, heat_cap, conduct,
    ask, wanted, wanted_at, places_v, blocks_v, asked, places, blocks,
    rows, fetched, out_rows,
    src, cond, inv, ga, gr, gl, edge, dir_a, dir_b, res, pot, power,
    local_sem, ask_send, ask_recv, row_send, row_recv, pow_send, pow_recv,
    halo_send, halo_recv,
):
    n = layers * blks
    ca, cr, lanes = source.shape
    cap = fetched.shape[0] // n
    stride = cap + 8
    ext_r = cr + 2 * ROWS
    blk, layer = lax.axis_index("blk"), lax.axis_index("layer")
    me = blk * layers + layer

    def flip(x, mask, size):
        total, bit = 0, 1
        while bit < size:
            total = total + bit * lax.rem(lax.div(x, bit) + lax.div(mask, bit), 2)
            bit *= 2
        return total

    def others(body):
        def step(i, carry):
            i = n - i
            k = lax.div(i, layers)
            to_blk = flip(blk, k, blks)
            to_layer = flip(layer, lax.rem(i, layers), layers)
            body((to_blk, to_layer), to_blk * layers + to_layer)
            return carry

        lax.fori_loop(1, n, step, 0)

    barrier = pltpu.get_barrier_semaphore()
    others(lambda at, j: pl.semaphore_signal(barrier, inc=1, device_id=at, device_id_type=MESH))

    def local(src_ref, dst_ref, i):
        copy = pltpu.make_async_copy(src_ref, dst_ref, local_sem.at[i])
        copy.start()
        return copy

    get_owner = local(owner_in, owner, 0)
    get_slot = local(slot_in, slot, 1)
    get_src = local(source, src.at[pl.ds(WIDE, ca), pl.ds(ROWS, cr)], 2)
    get_old = local(old_in, temp_old, 3)
    get_sigma = local(sigma_in, sigma, 4)
    get_cap = local(cap_in, heat_cap, 5)
    get_conduct = local(conduct_in, conduct, 6)

    get_owner.wait()
    get_slot.wait()
    route(owner, slot, ask, places_v, blocks_v, cap)
    own_ask = local(ask.at[me], wanted.at[me], 0)
    set_places = local(places_v, places, 1)
    set_blocks = local(blocks_v, blocks, 7)
    get_src.wait()

    pl.semaphore_wait(barrier, n - 1)

    def remote(src_ref, dst_ref, send, recv, at):
        return pltpu.make_async_remote_copy(
            src_ref=src_ref, dst_ref=dst_ref, send_sem=send, recv_sem=recv,
            device_id=at, device_id_type=MESH,
        )

    def ask_copy(at, j, at_slot):
        return remote(ask.at[j], wanted.at[at_slot], ask_send.at[j], ask_recv.at[at_slot], at)

    others(lambda at, j: ask_copy(at, j, me).start())

    def halo(kind, d, field):
        step_a, step_r = DIRECTIONS[d]
        deep = 3 + kind if step_r == 0 else 2 + kind
        count_a = ca if step_a == 0 else deep
        count_r = cr if step_r == 0 else EDGE
        from_a = {0: WIDE, 1: WIDE + ca - deep, -1: WIDE}[step_a]
        to_a = {0: WIDE, 1: WIDE - deep, -1: WIDE + ca}[step_a]
        from_r = {0: ROWS, 1: ROWS + cr - EDGE, -1: ROWS}[step_r]
        to_r = {0: ROWS, 1: ROWS - EDGE, -1: ROWS + cr}[step_r]
        return remote(
            field.at[pl.ds(from_a, count_a), pl.ds(from_r, count_r)],
            field.at[pl.ds(to_a, count_a), pl.ds(to_r, count_r)],
            halo_send.at[kind, d], halo_recv.at[kind, d],
            (lax.rem(blk + step_r + blks, blks), lax.rem(layer + step_a + layers, layers)),
        )

    def halo_all(kind, field, verb, chosen):
        for d in chosen:
            step_a = DIRECTIONS[d][0]
            if verb == "recv":
                step_a = -step_a

            def act(d=d):
                copy = halo(kind, d, field)
                {"start": copy.start, "recv": copy.wait_recv, "send": copy.wait_send}[verb]()

            if step_a == 0:
                act()
            else:
                pl.when(layer < layers - 1 if step_a > 0 else layer > 0)(act)

    every = range(len(DIRECTIONS))
    around_r = [d for d in every if DIRECTIONS[d][1] != 0]
    along_a = [d for d in every if DIRECTIONS[d][1] == 0]
    halo_all(0, src, "start", every)

    @pl.when(layer == 0)
    def _():
        cond[0:WIDE] = jnp.zeros((WIDE, ext_r, lanes), jnp.float32)

    @pl.when(layer == layers - 1)
    def _():
        cond[WIDE + ca :] = jnp.zeros((WIDE, ext_r, lanes), jnp.float32)

    own_ask.wait()
    others(lambda at, j: ask_copy(at, j, j).wait_recv())
    wanted_at[...] = jnp.clip(wanted[...] - 1, 0, temp_old.shape[0] - 1)
    local(wanted_at, asked, 0).wait()
    get_old.wait()

    def row_copy(at, j, at_slot):
        return remote(
            rows.at[pl.ds(pl.multiple_of(j * cap, 8), cap)],
            fetched.at[pl.ds(pl.multiple_of(at_slot * cap, 8), cap)],
            row_send.at[j], row_recv.at[at_slot], at,
        )

    def fill(target, start, table, j, origin):
        for c in range(cap):
            target[pl.ds(start + c, 1), :] = origin[pl.ds(table[j, 0, c], 1), :]

    def reply(at, j):
        fill(rows, pl.multiple_of(j * cap, 8), asked, j, temp_old)
        row_copy(at, j, me).start()

    others(reply)
    fill(fetched, pl.multiple_of(me * cap, 8), asked, me, temp_old)

    invert(wanted, where_v, stride)
    set_where = local(where_v, where_from, 0)
    get_cap.wait()
    get_conduct.wait()
    lane = iota((64, lanes), 1)

    def coefficients(b, carry):
        at = pl.ds(pl.multiple_of(b * 64, 8), 64)
        k = conduct[at, :]
        right = jnp.where(lane == lanes - 1, 0.0, 0.5 * (k + pltpu.roll(k, lanes - 1, 1)))
        left = jnp.where(lane == 0, 0.0, 0.5 * (k + pltpu.roll(k, 1, 1)))
        held = heat_cap[at, :]
        inverse = 1.0 / (held + left + right)
        old = temp_old[at, :]
        left = left * inverse
        right = right * inverse
        still = held * old * inverse
        inv_d[at, :] = inverse
        base[at, :] = still
        left_n[at, :] = left
        right_n[at, :] = right
        first_t[at, :] = still + left * pltpu.roll(old, 1, 1) + right * pltpu.roll(old, lanes - 1, 1)
        return carry

    lax.fori_loop(0, temp_old.shape[0] // 64, coefficients, 0)
    set_places.wait()
    set_blocks.wait()
    get_sigma.wait()

    others(lambda at, j: row_copy(at, j, j).wait_recv())

    def place(a, tiles):
        for t in tiles:
            for r in range(8 * t, 8 * t + 8):
                cond[WIDE + a, pl.ds(ROWS + r, 1), :] = fetched[pl.ds(places[a, 0, r], 1), :]
        for t in tiles:
            at = pl.ds(ROWS + 8 * t, 8)
            cond[WIDE + a, at, :] = sigma[a, pl.ds(8 * t, 8), :] / (1.0 + COUPLE * cond[WIDE + a, at, :])

    tiles = cr // 8

    def place_edges(a, carry):
        place(a, (0, tiles - 1))
        return carry

    def place_middle(a, carry):
        place(a, range(1, tiles - 1))
        return carry

    lax.fori_loop(0, ca, place_edges, 0)
    halo_all(1, cond, "start", around_r)
    lax.fori_loop(0, WIDE, place_middle, 0)
    lax.fori_loop(ca - WIDE, ca, place_middle, 0)
    halo_all(1, cond, "start", along_a)
    lax.fori_loop(WIDE, ca - WIDE, place_middle, 0)

    halo_all(0, src, "recv", every)
    halo_all(1, cond, "recv", every)

    def inside(e, values):
        at = layer * ca + e - WIDE
        return jnp.where(jnp.logical_and(at >= 0, at < layers * ca), values, 0.0)

    ratio = THETA / DELTA
    rho = [1.0 / ratio]
    for _ in range(2):
        rho.append(1.0 / (2.0 * ratio - rho[-1]))
    place_lane = iota((ext_r, lanes), 1)
    last = place_lane == lanes - 1
    ends = jnp.logical_or(place_lane == 0, last)

    def next_r(x):
        return pltpu.roll(x, ext_r - 1, 0)

    def back_r(x):
        return pltpu.roll(x, 1, 0)

    def next_l(x):
        return pltpu.roll(x, lanes - 1, 1)

    def back_l(x):
        return pltpu.roll(x, 1, 1)

    def first(e, carry):
        here = 0.5 * cond[e]
        up = here + 0.5 * cond[e + 1]
        down = here + 0.5 * cond[e - 1]
        along_r = here + next_r(here)
        along_l = jnp.where(last, 0.0, here + next_l(here))
        border = jnp.where(ends, here, 0.0)
        diag = up + down + along_r + back_r(along_r) + along_l + back_l(along_l) + border
        ga[e] = up
        gr[e] = along_r
        gl[e] = along_l
        edge[e] = border
        inverse = 1.0 / diag
        inv[e] = inverse
        dir_a[e] = inside(e, inverse * src[e] * (1.0 / THETA))
        return carry

    lax.fori_loop(1, 2 * WIDE + ca - 1, first, 0, unroll=2)

    def operate(field, e):
        v = field[e]
        flow_r = gr[e] * (v - next_r(v))
        flow_l = gl[e] * (v - next_l(v))
        result = ga[e] * (v - field[e + 1]) + ga[e - 1] * (v - field[e - 1])
        result = result + (flow_r - back_r(flow_r)) + (flow_l - back_l(flow_l))
        return v, result + edge[e] * v

    def second(e, carry):
        v, applied = operate(dir_a, e)
        rest = src[e] - applied
        res[e] = rest
        step = inside(e, (rho[1] * rho[0]) * v + (2.0 * rho[1] / DELTA) * (inv[e] * rest))
        dir_b[e] = step
        pot[e] = v + step
        return carry

    lax.fori_loop(2, 2 * WIDE + ca - 2, second, 0, unroll=2)

    def third(e, carry):
        v, applied = operate(dir_b, e)
        rest = res[e] - applied
        step = inside(e, (rho[2] * rho[1]) * v + (2.0 * rho[2] / DELTA) * (inv[e] * rest))
        pot[e] = pot[e] + step
        return carry

    lax.fori_loop(3, 2 * WIDE + ca - 3, third, 0, unroll=2)

    def joule(a, total):
        e = a + WIDE
        v = pot[e]
        up = v - pot[e + 1]
        down = v - pot[e - 1]
        gap_r = v - next_r(v)
        gap_l = v - next_l(v)
        gap_r = gap_r * gap_r
        gap_l = jnp.where(last, 0.0, gap_l * gap_l)
        border = jnp.where(ends, v * v, 0.0)
        result = up * up + down * down + gap_r + back_r(gap_r) + gap_l + back_l(gap_l) + border
        result = 0.5 * cond[e] * result
        power[pl.ds(pl.multiple_of(a * cr, 8), cr), :] = result[ROWS : ROWS + cr]
        potential[a] = v[ROWS : ROWS + cr]
        return total + result[ROWS : ROWS + cr]

    total = lax.fori_loop(0, ca, joule, jnp.zeros((cr, lanes), jnp.float32), unroll=2)
    part = jnp.sum(total, axis=0, keepdims=True)

    def pow_copy(at, j, at_slot):
        return remote(
            out_rows.at[pl.ds(pl.multiple_of(j * stride, 8), cap + 1)],
            arrived.at[pl.ds(pl.multiple_of(at_slot * stride, 8), cap + 1)],
            pow_send.at[j], pow_recv.at[at_slot], at,
        )

    def send_power(at, j):
        start = pl.multiple_of(j * stride, 8)
        fill(out_rows, start, blocks, j, power)
        out_rows[pl.ds(start + cap, 1), :] = part
        pow_copy(at, j, me).start()

    others(send_power)
    start = pl.multiple_of(me * stride, 8)
    fill(arrived, start, blocks, me, power)
    arrived[pl.ds(start + cap, 1), :] = part

    halo_all(0, src, "send", every)
    halo_all(1, cond, "send", every)

    def sent(at, j):
        ask_copy(at, j, j).wait_send()
        row_copy(at, j, j).wait_send()

    others(sent)
    set_where.wait()
    others(lambda at, j: pow_copy(at, j, j).wait_recv())

    def add(j, total):
        return total + arrived[pl.ds(j * stride + cap, 1), :]

    sums[...] = lax.fori_loop(0, n, add, jnp.zeros((1, lanes), jnp.float32), unroll=8)

    def gather(b, carry):
        for c in range(32):
            heat[pl.ds(b * 32 + c, 1), :] = arrived[pl.ds(where_from[b, 0, c], 1), :]
        return carry

    lax.fori_loop(0, where_from.shape[0], gather, 0, unroll=2)
    others(lambda at, j: pow_copy(at, j, j).wait_send())


def thermal_kernel(
    scale, potential_in, heat, sums, inv_d, base, first_t, left_n, right_n,
    potential, temp_out, temp_new, sem,
):
    through = pltpu.make_async_copy(potential_in, potential, sem.at[0])
    through.start()
    count, lanes = heat.shape
    factor = scale / jnp.sum(sums[...])
    step, pieces = 64, 4
    chunk = count // pieces

    def put(q):
        at = pl.ds(q * chunk, chunk)
        return pltpu.make_async_copy(temp_new.at[at], temp_out.at[at], sem.at[1 + q])

    def solve(b, carry):
        at = pl.ds(pl.multiple_of(b * step, 8), step)
        warm = heat[at, :] * factor * inv_d[at, :]
        current = first_t[at, :] + warm
        for _ in range(JACOBI - 1):
            before = pltpu.roll(current, 1, 1)
            after = pltpu.roll(current, lanes - 1, 1)
            current = (base[at, :] + warm) + left_n[at, :] * before + right_n[at, :] * after
        temp_new[at, :] = current
        return carry

    for q in range(pieces):
        lax.fori_loop(q * chunk // step, (q + 1) * chunk // step, solve, 0)
        put(q).start()
    for q in range(pieces):
        put(q).wait()
    through.wait()


def per_device(source, sigma_ref, owner, slot, temp_old, heat_cap, conduct):
    layers, blks = lax.axis_size("layer"), lax.axis_size("blk")
    n = layers * blks
    ca, cr, lanes = source.shape
    count = temp_old.shape[0]
    cap = 2 * ca * cr // n
    stride = cap + 8
    whole, vmem = pl.BlockSpec(memory_space=pl.ANY), pl.BlockSpec(memory_space=pltpu.VMEM)

    def f32(*shape):
        return pltpu.VMEM(shape, jnp.float32)

    def i32(*shape):
        return pltpu.VMEM(shape, jnp.int32)

    field = f32(ca + 2 * WIDE, cr + 2 * ROWS, lanes)
    each = pltpu.SemaphoreType.DMA((n,))
    thermal = jax.ShapeDtypeStruct(temp_old.shape, jnp.float32)

    def exchange(*refs):
        exchange_kernel(layers, blks, *refs)

    inputs = [
        pltpu.with_memory_space_constraint(x, pltpu.HBM)
        for x in (source, sigma_ref, owner, slot, temp_old, heat_cap, conduct)
    ]
    potential = jax.ShapeDtypeStruct(source.shape, jnp.float32)
    row = jax.ShapeDtypeStruct((1, lanes), jnp.float32)
    results = pl.pallas_call(
        exchange,
        out_shape=(potential, thermal, row) + (thermal,) * 5,
        in_specs=[whole] * 7,
        out_specs=(vmem,) * 8,
        scratch_shapes=[
            f32(n * stride, lanes),
            i32(count // 32, 1, LANES), pltpu.SMEM((count // 32, 1, LANES), jnp.int32),
            i32(ca, cr), i32(ca, cr), f32(ca, cr, lanes),
            f32(count, lanes), f32(count, lanes), f32(count, lanes),
            i32(n, 1, LANES), i32(n, 1, LANES), i32(n, 1, LANES),
            i32(ca, 1, LANES), i32(n, 1, LANES),
            pltpu.SMEM((n, 1, LANES), jnp.int32),
            pltpu.SMEM((ca, 1, LANES), jnp.int32),
            pltpu.SMEM((n, 1, LANES), jnp.int32),
            f32(n * cap, lanes), f32(n * cap, lanes), f32(n * stride, lanes),
            field, field, field, field, field, field, field, field, field, field, field,
            f32(ca * cr, lanes),
            pltpu.SemaphoreType.DMA((8,)),
            each, each, each, each, each, each,
            pltpu.SemaphoreType.DMA((2, 8)),
            pltpu.SemaphoreType.DMA((2, 8)),
        ],
        compiler_params=pltpu.CompilerParams(
            collective_id=0, has_side_effects=True, vmem_limit_bytes=40 << 20
        ),
    )(*inputs)

    def heat_step(*refs):
        thermal_kernel(float(source.size * n), *refs)

    return pl.pallas_call(
        heat_step,
        out_shape=(potential, thermal),
        in_specs=[whole] + [vmem] * 7,
        out_specs=(whole,) * 2,
        scratch_shapes=[f32(count, lanes), pltpu.SemaphoreType.DMA((5,))],
        compiler_params=pltpu.CompilerParams(vmem_limit_bytes=24 << 20),
    )(*results)


def solution(mesh):
    field = P("layer", "blk", None)
    index = P("layer", "blk")
    thermal = P(("blk", "layer"), None)
    return jax.shard_map(
        per_device,
        mesh=mesh,
        in_specs=(field, field, index, index, thermal, thermal, thermal),
        out_specs=(field, thermal),
        check_vma=False,
    )
```

```python
import jax
import jax.numpy as jnp
from jax import lax
from jax.experimental import pallas as pl
from jax.experimental.pallas import tpu as pltpu
from jax.sharding import PartitionSpec as P

JACOBI = 2
COUPLE = 0.4
THETA = 1.125
DELTA = 0.875

WIDE = 4
ROWS = 12
FROM = 8
EDGE = 4
LANES = 128
MESH = pl.DeviceIdType.MESH
DIRECTIONS = [(a, r) for r in (-1, 1, 0) for a in (-1, 1, 0) if (a, r) != (0, 0)]


def iota(shape, axis):
    return lax.broadcasted_iota(jnp.int32, shape, axis)


def ones(mask):
    return jnp.where(mask, 1.0, 0.0)


def dot(x, y, over):
    return lax.dot_general(
        x.astype(jnp.bfloat16), y.astype(jnp.bfloat16), (over, ((), ())),
        preferred_element_type=jnp.float32,
    )


def route(owner, slot, ask, places, blocks, cap):
    ca, cr = owner.shape
    n = ask.shape[0]
    earlier = ones(iota((cr, cr), 0) < iota((cr, cr), 1))
    seen = jnp.zeros((n, 1), jnp.float32)
    table = jnp.zeros((4 * n, LANES), jnp.float32)
    lane = iota((n, cr), 1).astype(jnp.float32)
    places[...] = jnp.zeros(places.shape, jnp.int32)
    for a in range(ca):
        name = owner[a : a + 1, :]
        mine = ones(iota((n, cr), 0) == name)
        before = dot(mine, earlier, ((1,), (0,))) + seen
        within = jnp.sum(mine * before, axis=0, keepdims=True).astype(jnp.int32)
        seen = seen + jnp.sum(mine, axis=1, keepdims=True)
        places[a, :, 0:cr] = jnp.clip(name * cap + within, 0, n * cap - 1)
        here = ones(iota((LANES, cr), 0) == within)
        code = slot[a : a + 1, :] + 1
        high = (code >> 5).astype(jnp.float32)
        low = (code & 31).astype(jnp.float32)
        digits = jnp.concatenate([mine * high, mine * low, mine * float(a), mine * lane], axis=0)
        table = table + dot(digits, here, ((1,), (1,)))
    codes = (table[0:n] * 32.0 + table[n : 2 * n]).astype(jnp.int32)
    block = (table[2 * n : 3 * n] * float(cr) + table[3 * n :]).astype(jnp.int32)
    for j in range(n):
        ask[j] = codes[j : j + 1]
        blocks[j] = jnp.clip(block[j : j + 1], 0, ca * cr - 1)


def invert(wanted, where_from, stride):
    n = wanted.shape[0]
    hn = where_from.shape[0]
    ln = 32

    def body(j, table):
        code = wanted[j] - 1
        at = ones(iota((hn, LANES), 0) == (code >> 5))
        low = ones(iota((ln, LANES), 0) == (code & 31))
        lane = iota((hn, LANES), 1).astype(jnp.float32)
        digits = jnp.concatenate([at * j.astype(jnp.float32), at * lane], axis=0)
        return table + dot(digits, low, ((1,), (1,)))

    table = lax.fori_loop(0, n, body, jnp.zeros((2 * hn, ln), jnp.float32), unroll=4)
    found = (table[:hn] * float(stride) + table[hn:]).astype(jnp.int32)
    found = jnp.clip(found, 0, n * stride - 1)
    where_from[...] = jnp.zeros(where_from.shape, jnp.int32)
    for h in range(hn):
        where_from[h, :, 0:ln] = found[h : h + 1]


def exchange_kernel(
    layers, blks,
    source, sigma_in, owner_in, slot_in, old_in, cap_in, conduct_in,
    potential, heat, sums, inv_d, base, first_t, left_n, right_n,
    arrived, where_v, where_from,
    owner, slot, sigma, temp_old, heat_cap, conduct,
    ask, wanted, wanted_at, places_v, blocks_v, asked, places, blocks,
    rows, fetched, out_rows,
    src, cond, inv, gr, gl, dir_a, wa, dir_b, wb, res, pot, temps, power,
    local_sem, ask_send, ask_recv, row_send, row_recv, pow_send, pow_recv,
    halo_send, halo_recv,
):
    n = layers * blks
    ca, cr, lanes = source.shape
    cap = fetched.shape[0] // n
    stride = cap + 8
    ext_r = cr + 2 * ROWS
    tall = cr + 2 * EDGE
    blk, layer = lax.axis_index("blk"), lax.axis_index("layer")
    me = blk * layers + layer

    def flip(x, mask, size):
        total, bit = 0, 1
        while bit < size:
            total = total + bit * lax.rem(lax.div(x, bit) + lax.div(mask, bit), 2)
            bit *= 2
        return total

    def others(body):
        def step(i, carry):
            i = n - i
            k = lax.div(i, layers)
            to_blk = flip(blk, k, blks)
            to_layer = flip(layer, lax.rem(i, layers), layers)
            body((to_blk, to_layer), to_blk * layers + to_layer)
            return carry

        lax.fori_loop(1, n, step, 0)

    barrier = pltpu.get_barrier_semaphore()
    others(lambda at, j: pl.semaphore_signal(barrier, inc=1, device_id=at, device_id_type=MESH))

    def local(src_ref, dst_ref, i):
        copy = pltpu.make_async_copy(src_ref, dst_ref, local_sem.at[i])
        copy.start()
        return copy

    get_owner = local(owner_in, owner, 0)
    get_slot = local(slot_in, slot, 1)
    get_src = local(source, src.at[pl.ds(WIDE, ca), pl.ds(ROWS, cr)], 2)
    get_old = local(old_in, temp_old, 3)
    get_sigma = local(sigma_in, sigma, 4)
    get_cap = local(cap_in, heat_cap, 5)
    get_conduct = local(conduct_in, conduct, 6)

    get_owner.wait()
    get_slot.wait()
    route(owner, slot, ask, places_v, blocks_v, cap)
    own_ask = local(ask.at[me], wanted.at[me], 0)
    set_places = local(places_v, places, 1)
    set_blocks = local(blocks_v, blocks, 7)
    get_src.wait()

    pl.semaphore_wait(barrier, n - 1)

    def remote(src_ref, dst_ref, send, recv, at):
        return pltpu.make_async_remote_copy(
            src_ref=src_ref, dst_ref=dst_ref, send_sem=send, recv_sem=recv,
            device_id=at, device_id_type=MESH,
        )

    def ask_copy(at, j, at_slot):
        return remote(ask.at[j], wanted.at[at_slot], ask_send.at[j], ask_recv.at[at_slot], at)

    others(lambda at, j: ask_copy(at, j, me).start())

    def halo(kind, d, field):
        step_a, step_r = DIRECTIONS[d]
        deep = 3 + kind if step_r == 0 else 2 + kind
        count_a = ca if step_a == 0 else deep
        count_r = cr if step_r == 0 else EDGE
        from_a = {0: WIDE, 1: WIDE + ca - deep, -1: WIDE}[step_a]
        to_a = {0: WIDE, 1: WIDE - deep, -1: WIDE + ca}[step_a]
        from_r = {0: ROWS, 1: ROWS + cr - EDGE, -1: ROWS}[step_r]
        to_r = {0: ROWS, 1: ROWS - EDGE, -1: ROWS + cr}[step_r]
        return remote(
            field.at[pl.ds(from_a, count_a), pl.ds(from_r, count_r)],
            field.at[pl.ds(to_a, count_a), pl.ds(to_r, count_r)],
            halo_send.at[kind, d], halo_recv.at[kind, d],
            (lax.rem(blk + step_r + blks, blks), lax.rem(layer + step_a + layers, layers)),
        )

    def halo_all(kind, field, verb, chosen):
        for d in chosen:
            step_a = DIRECTIONS[d][0]
            if verb == "recv":
                step_a = -step_a

            def act(d=d):
                copy = halo(kind, d, field)
                {"start": copy.start, "recv": copy.wait_recv, "send": copy.wait_send}[verb]()

            if step_a == 0:
                act()
            else:
                pl.when(layer < layers - 1 if step_a > 0 else layer > 0)(act)

    every = range(len(DIRECTIONS))
    around_r = [d for d in every if DIRECTIONS[d][1] != 0]
    along_a = [d for d in every if DIRECTIONS[d][1] == 0]
    halo_all(0, src, "start", every)

    def clear(start):
        empty = jnp.zeros((WIDE, ext_r, lanes), jnp.float32)
        for field in (cond, dir_a, wa, dir_b, wb, pot):
            field[pl.ds(start, WIDE)] = empty

    pl.when(layer == 0)(lambda: clear(0))
    pl.when(layer == layers - 1)(lambda: clear(WIDE + ca))

    own_ask.wait()
    others(lambda at, j: ask_copy(at, j, j).wait_recv())
    wanted_at[...] = jnp.clip(wanted[...] - 1, 0, temp_old.shape[0] - 1)
    local(wanted_at, asked, 0).wait()
    get_old.wait()

    def row_copy(at, j, at_slot):
        return remote(
            rows.at[pl.ds(pl.multiple_of(j * cap, 8), cap)],
            fetched.at[pl.ds(pl.multiple_of(at_slot * cap, 8), cap)],
            row_send.at[j], row_recv.at[at_slot], at,
        )

    def fill(target, start, table, j, origin):
        for c in range(cap):
            target[pl.ds(start + c, 1), :] = origin[pl.ds(table[j, 0, c], 1), :]

    def reply(at, j):
        fill(rows, pl.multiple_of(j * cap, 8), asked, j, temp_old)
        row_copy(at, j, me).start()

    others(reply)
    fill(fetched, pl.multiple_of(me * cap, 8), asked, me, temp_old)

    invert(wanted, where_v, stride)
    set_where = local(where_v, where_from, 0)
    get_cap.wait()
    get_conduct.wait()
    lane = iota((64, lanes), 1)

    def coefficients(b, carry):
        at = pl.ds(pl.multiple_of(b * 64, 8), 64)
        k = conduct[at, :]
        right = jnp.where(lane == lanes - 1, 0.0, 0.5 * (k + pltpu.roll(k, lanes - 1, 1)))
        left = jnp.where(lane == 0, 0.0, 0.5 * (k + pltpu.roll(k, 1, 1)))
        held = heat_cap[at, :]
        inverse = 1.0 / (held + left + right)
        old = temp_old[at, :]
        left = left * inverse
        right = right * inverse
        still = held * old * inverse
        inv_d[at, :] = inverse
        base[at, :] = still
        left_n[at, :] = left
        right_n[at, :] = right
        first_t[at, :] = still + left * pltpu.roll(old, 1, 1) + right * pltpu.roll(old, lanes - 1, 1)
        return carry

    lax.fori_loop(0, temp_old.shape[0] // 64, coefficients, 0)
    set_places.wait()
    set_blocks.wait()
    get_sigma.wait()

    others(lambda at, j: row_copy(at, j, j).wait_recv())

    def place(a, tiles):
        for t in tiles:
            for r in range(8 * t, 8 * t + 8):
                temps[a, r : r + 1, :] = fetched[pl.ds(places[a, 0, r], 1), :]
        for t in tiles:
            at = pl.ds(8 * t, 8)
            half = 0.5 * sigma[a, at, :] / (1.0 + COUPLE * temps[a, at, :])
            cond[WIDE + a, pl.ds(ROWS + 8 * t, 8), :] = half

    tiles = cr // 8

    def place_edges(a, carry):
        place(a, (0, tiles - 1))
        return carry

    def place_middle(a, carry):
        place(a, range(1, tiles - 1))
        return carry

    lax.fori_loop(0, ca, place_edges, 0)
    halo_all(1, cond, "start", around_r)
    lax.fori_loop(0, WIDE, place_middle, 0)
    lax.fori_loop(ca - WIDE, ca, place_middle, 0)
    halo_all(1, cond, "start", along_a)
    lax.fori_loop(WIDE, ca - WIDE, place_middle, 0)

    halo_all(0, src, "recv", every)
    halo_all(1, cond, "recv", every)

    ratio = THETA / DELTA
    rho = [1.0 / ratio]
    for _ in range(2):
        rho.append(1.0 / (2.0 * ratio - rho[-1]))
    lane_here = iota((tall, lanes), 1)
    at_first, at_last = lane_here == 0, lane_here == lanes - 1

    def next_l(x):
        return pltpu.roll(x, lanes - 1, 1)

    def back_l(x):
        return pltpu.roll(x, 1, 1)

    def beside(field, e, r):
        up, down = field[e + 1, pl.ds(r, tall), :], field[e - 1, pl.ds(r, tall), :]
        after = field[e, pl.ds(r + 1, tall), :]
        before = field[e, pl.ds(r - 1, tall), :]
        return (up + down) + (after + before)

    def sweep(body, reach):
        def slab(e, carry):
            body(e, FROM)
            return carry

        lax.fori_loop(WIDE, WIDE + ca, slab, 0, unroll=8)

        @pl.when(layer > 0)
        def _():
            lax.fori_loop(WIDE - reach, WIDE, slab, 0, unroll=True)

        @pl.when(layer < layers - 1)
        def _():
            lax.fori_loop(WIDE + ca, WIDE + ca + reach, slab, 0, unroll=True)

    def first(e, r):
        at = pl.ds(r, tall)
        here = cond[e, at, :]
        right = here + next_l(here)
        left = here + back_l(here)
        diag = (4.0 * here + beside(cond, e, r)) + (
            jnp.where(at_last, here, right) + jnp.where(at_first, here, left)
        )
        inverse = 1.0 / diag
        step = (inverse * src[e, at, :]) * (1.0 / THETA)
        gr[e, at, :] = jnp.where(at_last, 0.0, right)
        gl[e, at, :] = jnp.where(at_first, 0.0, left)
        inv[e, at, :] = inverse
        dir_a[e, at, :] = step
        wa[e, at, :] = here * step

    def pulls(field, weighted, e, r, v, here):
        at = pl.ds(r, tall)
        sideways = gr[e, at, :] * next_l(v) + gl[e, at, :] * back_l(v)
        return (here * beside(field, e, r) + beside(weighted, e, r)) + sideways

    def second(e, r):
        at = pl.ds(r, tall)
        v, here = dir_a[e, at, :], cond[e, at, :]
        rest = inv[e, at, :] * (src[e, at, :] + pulls(dir_a, wa, e, r, v, here)) - v
        step = (rho[1] * rho[0]) * v + (2.0 * rho[1] / DELTA) * rest
        res[e, at, :] = rest
        dir_b[e, at, :] = step
        wb[e, at, :] = here * step

    def third(e, r):
        at = pl.ds(r, tall)
        v, here = dir_b[e, at, :], cond[e, at, :]
        rest = res[e, at, :] + inv[e, at, :] * pulls(dir_b, wb, e, r, v, here) - v
        step = (rho[2] * rho[1]) * v + (2.0 * rho[2] / DELTA) * rest
        pot[e, at, :] = dir_a[e, at, :] + v + step

    sweep(first, 3)
    sweep(second, 2)
    sweep(third, 1)

    core_lane = iota((cr, lanes), 1)
    core_first, core_last = core_lane == 0, core_lane == lanes - 1

    def joule(a, total):
        e = a + WIDE

        def near(shift_e, shift_r):
            return pot[e + shift_e, pl.ds(ROWS + shift_r, cr), :]

        v = near(0, 0)
        gaps = [v - near(1, 0), v - near(-1, 0), v - near(0, 1), v - near(0, -1)]
        gaps.append(v - jnp.where(core_last, 0.0, next_l(v)))
        gaps.append(v - jnp.where(core_first, 0.0, back_l(v)))
        squares = [gap * gap for gap in gaps]
        result = (squares[0] + squares[1]) + (squares[2] + squares[3]) + (squares[4] + squares[5])
        result = cond[e, pl.ds(ROWS, cr), :] * result
        power[pl.ds(pl.multiple_of(a * cr, 8), cr), :] = result
        potential[a] = v
        return total + jnp.sum(result.reshape(cr // 8, 8, lanes), axis=0)

    total = lax.fori_loop(0, ca, joule, jnp.zeros((8, lanes), jnp.float32), unroll=8)
    part = jnp.sum(total, axis=0, keepdims=True)

    def pow_copy(at, j, at_slot):
        return remote(
            out_rows.at[pl.ds(pl.multiple_of(j * stride, 8), cap + 1)],
            arrived.at[pl.ds(pl.multiple_of(at_slot * stride, 8), cap + 1)],
            pow_send.at[j], pow_recv.at[at_slot], at,
        )

    def send_power(at, j):
        start = pl.multiple_of(j * stride, 8)
        fill(out_rows, start, blocks, j, power)
        out_rows[pl.ds(start + cap, 1), :] = part
        pow_copy(at, j, me).start()

    others(send_power)
    start = pl.multiple_of(me * stride, 8)
    fill(arrived, start, blocks, me, power)
    arrived[pl.ds(start + cap, 1), :] = part

    halo_all(0, src, "send", every)
    halo_all(1, cond, "send", every)

    def sent(at, j):
        ask_copy(at, j, j).wait_send()
        row_copy(at, j, j).wait_send()

    others(sent)
    set_where.wait()
    others(lambda at, j: pow_copy(at, j, j).wait_recv())

    def add(j, total):
        return total + arrived[pl.ds(j * stride + cap, 1), :]

    sums[...] = lax.fori_loop(0, n, add, jnp.zeros((1, lanes), jnp.float32), unroll=8)

    def gather(b, carry):
        for c in range(32):
            heat[pl.ds(b * 32 + c, 1), :] = arrived[pl.ds(where_from[b, 0, c], 1), :]
        return carry

    lax.fori_loop(0, where_from.shape[0], gather, 0, unroll=2)
    others(lambda at, j: pow_copy(at, j, j).wait_send())


def thermal_kernel(
    scale, potential_in, heat, sums, inv_d, base, first_t, left_n, right_n,
    potential, temp_out, temp_new, sem,
):
    through = pltpu.make_async_copy(potential_in, potential, sem.at[0])
    through.start()
    count, lanes = heat.shape
    factor = scale / jnp.sum(sums[...])
    step, pieces = 64, 4
    chunk = count // pieces

    def put(q):
        at = pl.ds(q * chunk, chunk)
        return pltpu.make_async_copy(temp_new.at[at], temp_out.at[at], sem.at[1 + q])

    def solve(b, carry):
        at = pl.ds(pl.multiple_of(b * step, 8), step)
        warm = heat[at, :] * factor * inv_d[at, :]
        current = first_t[at, :] + warm
        for _ in range(JACOBI - 1):
            before = pltpu.roll(current, 1, 1)
            after = pltpu.roll(current, lanes - 1, 1)
            current = (base[at, :] + warm) + left_n[at, :] * before + right_n[at, :] * after
        temp_new[at, :] = current
        return carry

    for q in range(pieces):
        lax.fori_loop(q * chunk // step, (q + 1) * chunk // step, solve, 0)
        put(q).start()
    for q in range(pieces):
        put(q).wait()
    through.wait()


def per_device(source, sigma_ref, owner, slot, temp_old, heat_cap, conduct):
    layers, blks = lax.axis_size("layer"), lax.axis_size("blk")
    n = layers * blks
    ca, cr, lanes = source.shape
    count = temp_old.shape[0]
    cap = 2 * ca * cr // n
    stride = cap + 8
    whole, vmem = pl.BlockSpec(memory_space=pl.ANY), pl.BlockSpec(memory_space=pltpu.VMEM)

    def f32(*shape):
        return pltpu.VMEM(shape, jnp.float32)

    def i32(*shape):
        return pltpu.VMEM(shape, jnp.int32)

    field = f32(ca + 2 * WIDE, cr + 2 * ROWS, lanes)
    each = pltpu.SemaphoreType.DMA((n,))
    thermal = jax.ShapeDtypeStruct(temp_old.shape, jnp.float32)

    def exchange(*refs):
        exchange_kernel(layers, blks, *refs)

    inputs = [
        pltpu.with_memory_space_constraint(x, pltpu.HBM)
        for x in (source, sigma_ref, owner, slot, temp_old, heat_cap, conduct)
    ]
    potential = jax.ShapeDtypeStruct(source.shape, jnp.float32)
    row = jax.ShapeDtypeStruct((1, lanes), jnp.float32)
    results = pl.pallas_call(
        exchange,
        out_shape=(potential, thermal, row) + (thermal,) * 5,
        in_specs=[whole] * 7,
        out_specs=(vmem,) * 8,
        scratch_shapes=[
            f32(n * stride, lanes),
            i32(count // 32, 1, LANES), pltpu.SMEM((count // 32, 1, LANES), jnp.int32),
            i32(ca, cr), i32(ca, cr), f32(ca, cr, lanes),
            f32(count, lanes), f32(count, lanes), f32(count, lanes),
            i32(n, 1, LANES), i32(n, 1, LANES), i32(n, 1, LANES),
            i32(ca, 1, LANES), i32(n, 1, LANES),
            pltpu.SMEM((n, 1, LANES), jnp.int32),
            pltpu.SMEM((ca, 1, LANES), jnp.int32),
            pltpu.SMEM((n, 1, LANES), jnp.int32),
            f32(n * cap, lanes), f32(n * cap, lanes), f32(n * stride, lanes),
            field, field, field, field, field, field, field, field, field, field, field,
            f32(ca, cr, lanes), f32(ca * cr, lanes),
            pltpu.SemaphoreType.DMA((8,)),
            each, each, each, each, each, each,
            pltpu.SemaphoreType.DMA((2, 8)),
            pltpu.SemaphoreType.DMA((2, 8)),
        ],
        compiler_params=pltpu.CompilerParams(
            collective_id=0, has_side_effects=True, vmem_limit_bytes=40 << 20
        ),
    )(*inputs)

    def heat_step(*refs):
        thermal_kernel(float(source.size * n), *refs)

    return pl.pallas_call(
        heat_step,
        out_shape=(potential, thermal),
        in_specs=[whole] + [vmem] * 7,
        out_specs=(whole,) * 2,
        scratch_shapes=[f32(count, lanes), pltpu.SemaphoreType.DMA((5,))],
        compiler_params=pltpu.CompilerParams(vmem_limit_bytes=24 << 20),
    )(*results)


def solution(mesh):
    field = P("layer", "blk", None)
    index = P("layer", "blk")
    thermal = P(("blk", "layer"), None)
    return jax.shard_map(
        per_device,
        mesh=mesh,
        in_specs=(field, field, index, index, thermal, thermal, thermal),
        out_specs=(field, thermal),
        check_vma=False,
    )
```

```python
import jax
import jax.numpy as jnp
from jax import lax
from jax.experimental import pallas as pl
from jax.experimental.pallas import tpu as pltpu
from jax.sharding import PartitionSpec as P

JACOBI = 2
COUPLE = 0.4
THETA = 1.125
DELTA = 0.875

WIDE = 4
ROWS = 12
FROM = 8
EDGE = 4
LANES = 128
MESH = pl.DeviceIdType.MESH
DIRECTIONS = [(a, r) for r in (-1, 1, 0) for a in (-1, 1, 0) if (a, r) != (0, 0)]


def iota(shape, axis):
    return lax.broadcasted_iota(jnp.int32, shape, axis)


def ones(mask):
    return jnp.where(mask, 1.0, 0.0)


def dot(x, y, over):
    return lax.dot_general(
        x.astype(jnp.bfloat16), y.astype(jnp.bfloat16), (over, ((), ())),
        preferred_element_type=jnp.float32,
    )


def route(owner, slot, ask, places, blocks, cap):
    ca, cr = owner.shape
    n = ask.shape[0]
    earlier = ones(iota((cr, cr), 0) < iota((cr, cr), 1))
    seen = jnp.zeros((n, 1), jnp.float32)
    table = jnp.zeros((4 * n, LANES), jnp.float32)
    lane = iota((n, cr), 1).astype(jnp.float32)
    places[...] = jnp.zeros(places.shape, jnp.int32)
    for a in range(ca):
        name = owner[a : a + 1, :]
        mine = ones(iota((n, cr), 0) == name)
        before = dot(mine, earlier, ((1,), (0,))) + seen
        within = jnp.sum(mine * before, axis=0, keepdims=True).astype(jnp.int32)
        seen = seen + jnp.sum(mine, axis=1, keepdims=True)
        places[a, :, 0:cr] = jnp.clip(name * cap + within, 0, n * cap - 1)
        here = ones(iota((LANES, cr), 0) == within)
        code = slot[a : a + 1, :] + 1
        high = (code >> 5).astype(jnp.float32)
        low = (code & 31).astype(jnp.float32)
        digits = jnp.concatenate([mine * high, mine * low, mine * float(a), mine * lane], axis=0)
        table = table + dot(digits, here, ((1,), (1,)))
    codes = (table[0:n] * 32.0 + table[n : 2 * n]).astype(jnp.int32)
    block = (table[2 * n : 3 * n] * float(cr) + table[3 * n :]).astype(jnp.int32)
    for j in range(n):
        ask[j] = codes[j : j + 1]
        blocks[j] = jnp.clip(block[j : j + 1], 0, ca * cr - 1)


def invert(wanted, where_from, stride):
    n = wanted.shape[0]
    hn = where_from.shape[0]
    ln = 32

    def body(j, table):
        code = wanted[j] - 1
        at = ones(iota((hn, LANES), 0) == (code >> 5))
        low = ones(iota((ln, LANES), 0) == (code & 31))
        lane = iota((hn, LANES), 1).astype(jnp.float32)
        digits = jnp.concatenate([at * j.astype(jnp.float32), at * lane], axis=0)
        return table + dot(digits, low, ((1,), (1,)))

    table = lax.fori_loop(0, n, body, jnp.zeros((2 * hn, ln), jnp.float32), unroll=4)
    found = (table[:hn] * float(stride) + table[hn:]).astype(jnp.int32)
    found = jnp.clip(found, 0, n * stride - 1)
    where_from[...] = jnp.zeros(where_from.shape, jnp.int32)
    for h in range(hn):
        where_from[h, :, 0:ln] = found[h : h + 1]


def exchange_kernel(
    layers, blks,
    source, sigma_in, owner_in, slot_in, old_in, cap_in, conduct_in,
    potential, heat, sums, inv_d, base, first_t, left_n, right_n,
    arrived, where_v, where_from,
    owner, slot, sigma, temp_old, heat_cap, conduct,
    ask, wanted, wanted_at, places_v, blocks_v, asked, places, blocks,
    rows, fetched, out_rows,
    src, cond, inv, gr, gl, dir_a, wa, dir_b, wb, res, pot, temps, power,
    local_sem, ask_send, ask_recv, row_send, row_recv, pow_send, pow_recv,
    halo_send, halo_recv,
):
    n = layers * blks
    ca, cr, lanes = source.shape
    cap = fetched.shape[0] // n
    stride = cap + 8
    ext_r = cr + 2 * ROWS
    tall = cr + 2 * EDGE
    blk, layer = lax.axis_index("blk"), lax.axis_index("layer")
    me = blk * layers + layer

    def flips(x, size):
        out, bit = [x], 1
        while bit < size:
            by = bit - 2 * bit * lax.rem(lax.div(x, bit), 2)
            out += [value + by for value in out]
            bit *= 2
        return out

    def flip(x, mask, size):
        total, bit = 0, 1
        while bit < size:
            total = total + bit * lax.rem(lax.div(x, bit) + lax.div(mask, bit), 2)
            bit *= 2
        return total

    to_layers = flips(layer, layers)
    to_blks = flips(blk, blks)

    def others(body):
        for to_blk in to_blks[::-1]:
            for to_layer in to_layers[::-1]:
                if to_blk is not blk or to_layer is not layer:
                    body((to_blk, to_layer), to_blk * layers + to_layer)

    def others_long(body):
        def step(i, carry):
            k = blks - 1 - i
            to_blk = flip(blk, k, blks)
            for to_layer in to_layers[::-1]:
                def go(to_layer=to_layer):
                    body((to_blk, to_layer), to_blk * layers + to_layer)

                if to_layer is layer:
                    pl.when(k > 0)(go)
                else:
                    go()
            return carry

        lax.fori_loop(0, blks, step, 0)

    barrier = pltpu.get_barrier_semaphore()
    others(lambda at, j: pl.semaphore_signal(barrier, inc=1, device_id=at, device_id_type=MESH))

    def local(src_ref, dst_ref, i):
        copy = pltpu.make_async_copy(src_ref, dst_ref, local_sem.at[i])
        copy.start()
        return copy

    get_owner = local(owner_in, owner, 0)
    get_slot = local(slot_in, slot, 1)
    get_src = local(source, src.at[pl.ds(WIDE, ca), pl.ds(ROWS, cr)], 2)
    get_old = local(old_in, temp_old, 3)
    get_sigma = local(sigma_in, sigma, 4)
    get_cap = local(cap_in, heat_cap, 5)
    get_conduct = local(conduct_in, conduct, 6)

    get_owner.wait()
    get_slot.wait()
    route(owner, slot, ask, places_v, blocks_v, cap)
    own_ask = local(ask.at[me], wanted.at[me], 0)
    set_places = local(places_v, places, 1)
    set_blocks = local(blocks_v, blocks, 7)
    get_src.wait()

    pl.semaphore_wait(barrier, n - 1)

    def remote(src_ref, dst_ref, send, recv, at):
        return pltpu.make_async_remote_copy(
            src_ref=src_ref, dst_ref=dst_ref, send_sem=send, recv_sem=recv,
            device_id=at, device_id_type=MESH,
        )

    def ask_copy(at, j, at_slot):
        return remote(ask.at[j], wanted.at[at_slot], ask_send.at[j], ask_recv.at[at_slot], at)

    others(lambda at, j: ask_copy(at, j, me).start())

    def halo(kind, d, field):
        step_a, step_r = DIRECTIONS[d]
        deep = 3 + kind if step_r == 0 else 2 + kind
        count_a = ca if step_a == 0 else deep
        count_r = cr if step_r == 0 else EDGE
        from_a = {0: WIDE, 1: WIDE + ca - deep, -1: WIDE}[step_a]
        to_a = {0: WIDE, 1: WIDE - deep, -1: WIDE + ca}[step_a]
        from_r = {0: ROWS, 1: ROWS + cr - EDGE, -1: ROWS}[step_r]
        to_r = {0: ROWS, 1: ROWS - EDGE, -1: ROWS + cr}[step_r]
        return remote(
            field.at[pl.ds(from_a, count_a), pl.ds(from_r, count_r)],
            field.at[pl.ds(to_a, count_a), pl.ds(to_r, count_r)],
            halo_send.at[kind, d], halo_recv.at[kind, d],
            (lax.rem(blk + step_r + blks, blks), lax.rem(layer + step_a + layers, layers)),
        )

    def halo_all(kind, field, verb, chosen):
        for d in chosen:
            step_a = DIRECTIONS[d][0]
            if verb == "recv":
                step_a = -step_a

            def act(d=d):
                copy = halo(kind, d, field)
                {"start": copy.start, "recv": copy.wait_recv, "send": copy.wait_send}[verb]()

            if step_a == 0:
                act()
            else:
                pl.when(layer < layers - 1 if step_a > 0 else layer > 0)(act)

    every = range(len(DIRECTIONS))
    around_r = [d for d in every if DIRECTIONS[d][1] != 0]
    along_a = [d for d in every if DIRECTIONS[d][1] == 0]
    halo_all(0, src, "start", every)

    def clear(start):
        empty = jnp.zeros((WIDE, ext_r, lanes), jnp.float32)
        for field in (cond, dir_a, wa, dir_b, wb, pot):
            field[pl.ds(start, WIDE)] = empty

    pl.when(layer == 0)(lambda: clear(0))
    pl.when(layer == layers - 1)(lambda: clear(WIDE + ca))

    own_ask.wait()
    others(lambda at, j: ask_copy(at, j, j).wait_recv())
    wanted_at[...] = jnp.clip(wanted[...] - 1, 0, temp_old.shape[0] - 1)
    local(wanted_at, asked, 0).wait()
    get_old.wait()

    def row_copy(at, j, at_slot):
        return remote(
            rows.at[pl.ds(pl.multiple_of(j * cap, 8), cap)],
            fetched.at[pl.ds(pl.multiple_of(at_slot * cap, 8), cap)],
            row_send.at[j], row_recv.at[at_slot], at,
        )

    def fill(target, start, table, j, origin):
        for c in range(cap):
            target[pl.ds(start + c, 1), :] = origin[pl.ds(table[j, 0, c], 1), :]

    def reply(at, j):
        fill(rows, pl.multiple_of(j * cap, 8), asked, j, temp_old)
        row_copy(at, j, me).start()

    others_long(reply)
    fill(fetched, pl.multiple_of(me * cap, 8), asked, me, temp_old)

    invert(wanted, where_v, stride)
    set_where = local(where_v, where_from, 0)
    get_cap.wait()
    get_conduct.wait()
    lane = iota((64, lanes), 1)

    def coefficients(b, carry):
        at = pl.ds(pl.multiple_of(b * 64, 8), 64)
        k = conduct[at, :]
        right = jnp.where(lane == lanes - 1, 0.0, 0.5 * (k + pltpu.roll(k, lanes - 1, 1)))
        left = jnp.where(lane == 0, 0.0, 0.5 * (k + pltpu.roll(k, 1, 1)))
        held = heat_cap[at, :]
        inverse = 1.0 / (held + left + right)
        old = temp_old[at, :]
        left = left * inverse
        right = right * inverse
        still = held * old * inverse
        inv_d[at, :] = inverse
        base[at, :] = still
        left_n[at, :] = left
        right_n[at, :] = right
        first_t[at, :] = still + left * pltpu.roll(old, 1, 1) + right * pltpu.roll(old, lanes - 1, 1)
        return carry

    lax.fori_loop(0, temp_old.shape[0] // 64, coefficients, 0)
    set_places.wait()
    set_blocks.wait()
    get_sigma.wait()

    others(lambda at, j: row_copy(at, j, j).wait_recv())

    def place(a, tiles):
        for t in tiles:
            for r in range(8 * t, 8 * t + 8):
                temps[a, r : r + 1, :] = fetched[pl.ds(places[a, 0, r], 1), :]
        for t in tiles:
            at = pl.ds(8 * t, 8)
            half = 0.5 * sigma[a, at, :] / (1.0 + COUPLE * temps[a, at, :])
            cond[WIDE + a, pl.ds(ROWS + 8 * t, 8), :] = half

    tiles = cr // 8

    def place_edges(a, carry):
        place(a, (0, tiles - 1))
        return carry

    def place_middle(a, carry):
        place(a, range(1, tiles - 1))
        return carry

    lax.fori_loop(0, ca, place_edges, 0, unroll=4)
    halo_all(1, cond, "start", around_r)
    lax.fori_loop(0, WIDE, place_middle, 0, unroll=2)
    lax.fori_loop(ca - WIDE, ca, place_middle, 0, unroll=2)
    halo_all(1, cond, "start", along_a)
    lax.fori_loop(WIDE, ca - WIDE, place_middle, 0, unroll=2)

    halo_all(0, src, "recv", every)
    halo_all(1, cond, "recv", every)

    ratio = THETA / DELTA
    rho = [1.0 / ratio]
    for _ in range(2):
        rho.append(1.0 / (2.0 * ratio - rho[-1]))
    lane_here = iota((tall, lanes), 1)
    at_first, at_last = lane_here == 0, lane_here == lanes - 1

    def next_l(x):
        return pltpu.roll(x, lanes - 1, 1)

    def back_l(x):
        return pltpu.roll(x, 1, 1)

    def beside(field, e, r):
        up, down = field[e + 1, pl.ds(r, tall), :], field[e - 1, pl.ds(r, tall), :]
        after = field[e, pl.ds(r + 1, tall), :]
        before = field[e, pl.ds(r - 1, tall), :]
        return (up + down) + (after + before)

    def sweep(body, reach):
        def slab(e, carry):
            body(e, FROM)
            return carry

        lax.fori_loop(WIDE, WIDE + ca, slab, 0, unroll=8)

        @pl.when(layer > 0)
        def _():
            lax.fori_loop(WIDE - reach, WIDE, slab, 0, unroll=True)

        @pl.when(layer < layers - 1)
        def _():
            lax.fori_loop(WIDE + ca, WIDE + ca + reach, slab, 0, unroll=True)

    def first(e, r):
        at = pl.ds(r, tall)
        here = cond[e, at, :]
        right = here + next_l(here)
        left = here + back_l(here)
        diag = (4.0 * here + beside(cond, e, r)) + (
            jnp.where(at_last, here, right) + jnp.where(at_first, here, left)
        )
        inverse = 1.0 / diag
        step = (inverse * src[e, at, :]) * (1.0 / THETA)
        gr[e, at, :] = jnp.where(at_last, 0.0, right)
        gl[e, at, :] = jnp.where(at_first, 0.0, left)
        inv[e, at, :] = inverse
        dir_a[e, at, :] = step
        wa[e, at, :] = here * step

    def pulls(field, weighted, e, r, v, here):
        at = pl.ds(r, tall)
        sideways = gr[e, at, :] * next_l(v) + gl[e, at, :] * back_l(v)
        return (here * beside(field, e, r) + beside(weighted, e, r)) + sideways

    def second(e, r):
        at = pl.ds(r, tall)
        v, here = dir_a[e, at, :], cond[e, at, :]
        rest = inv[e, at, :] * (src[e, at, :] + pulls(dir_a, wa, e, r, v, here)) - v
        step = (rho[1] * rho[0]) * v + (2.0 * rho[1] / DELTA) * rest
        res[e, at, :] = rest
        dir_b[e, at, :] = step
        wb[e, at, :] = here * step

    def third(e, r):
        at = pl.ds(r, tall)
        v, here = dir_b[e, at, :], cond[e, at, :]
        rest = res[e, at, :] + inv[e, at, :] * pulls(dir_b, wb, e, r, v, here) - v
        step = (rho[2] * rho[1]) * v + (2.0 * rho[2] / DELTA) * rest
        pot[e, at, :] = dir_a[e, at, :] + v + step

    sweep(first, 3)
    sweep(second, 2)
    sweep(third, 1)

    core_lane = iota((cr, lanes), 1)
    core_first, core_last = core_lane == 0, core_lane == lanes - 1

    def joule(a, total):
        e = a + WIDE

        def near(shift_e, shift_r):
            return pot[e + shift_e, pl.ds(ROWS + shift_r, cr), :]

        v = near(0, 0)
        gaps = [v - near(1, 0), v - near(-1, 0), v - near(0, 1), v - near(0, -1)]
        gaps.append(v - jnp.where(core_last, 0.0, next_l(v)))
        gaps.append(v - jnp.where(core_first, 0.0, back_l(v)))
        squares = [gap * gap for gap in gaps]
        result = (squares[0] + squares[1]) + (squares[2] + squares[3]) + (squares[4] + squares[5])
        result = cond[e, pl.ds(ROWS, cr), :] * result
        power[pl.ds(pl.multiple_of(a * cr, 8), cr), :] = result
        potential[a] = v
        return total + jnp.sum(result.reshape(cr // 8, 8, lanes), axis=0)

    total = lax.fori_loop(0, ca, joule, jnp.zeros((8, lanes), jnp.float32), unroll=8)
    part = jnp.sum(total, axis=0, keepdims=True)

    def pow_copy(at, j, at_slot):
        return remote(
            out_rows.at[pl.ds(pl.multiple_of(j * stride, 8), cap + 1)],
            arrived.at[pl.ds(pl.multiple_of(at_slot * stride, 8), cap + 1)],
            pow_send.at[j], pow_recv.at[at_slot], at,
        )

    def send_power(at, j):
        start = pl.multiple_of(j * stride, 8)
        fill(out_rows, start, blocks, j, power)
        out_rows[pl.ds(start + cap, 1), :] = part
        pow_copy(at, j, me).start()

    others_long(send_power)
    start = pl.multiple_of(me * stride, 8)
    fill(arrived, start, blocks, me, power)
    arrived[pl.ds(start + cap, 1), :] = part

    halo_all(0, src, "send", every)
    halo_all(1, cond, "send", every)

    def sent(at, j):
        ask_copy(at, j, j).wait_send()
        row_copy(at, j, j).wait_send()
        pow_copy(at, j, j).wait_send()

    others(sent)
    set_where.wait()
    others(lambda at, j: pow_copy(at, j, j).wait_recv())

    def add(j, total):
        return total + arrived[pl.ds(j * stride + cap, 1), :]

    sums[...] = lax.fori_loop(0, n, add, jnp.zeros((1, lanes), jnp.float32), unroll=8)

    def gather(b, carry):
        for c in range(32):
            heat[pl.ds(b * 32 + c, 1), :] = arrived[pl.ds(where_from[b, 0, c], 1), :]
        return carry

    lax.fori_loop(0, where_from.shape[0], gather, 0, unroll=4)


def thermal_kernel(
    scale, potential_in, heat, sums, inv_d, base, first_t, left_n, right_n,
    potential, temp_out, temp_new, sem,
):
    through = pltpu.make_async_copy(potential_in, potential, sem.at[0])
    through.start()
    count, lanes = heat.shape
    factor = scale / jnp.sum(sums[...])
    step, pieces = 64, 4
    chunk = count // pieces

    def put(q):
        at = pl.ds(q * chunk, chunk)
        return pltpu.make_async_copy(temp_new.at[at], temp_out.at[at], sem.at[1 + q])

    def solve(b, carry):
        at = pl.ds(pl.multiple_of(b * step, 8), step)
        warm = heat[at, :] * factor * inv_d[at, :]
        current = first_t[at, :] + warm
        for _ in range(JACOBI - 1):
            before = pltpu.roll(current, 1, 1)
            after = pltpu.roll(current, lanes - 1, 1)
            current = (base[at, :] + warm) + left_n[at, :] * before + right_n[at, :] * after
        temp_new[at, :] = current
        return carry

    for q in range(pieces):
        lax.fori_loop(q * chunk // step, (q + 1) * chunk // step, solve, 0, unroll=True)
        put(q).start()
    for q in range(pieces):
        put(q).wait()
    through.wait()


def per_device(source, sigma_ref, owner, slot, temp_old, heat_cap, conduct):
    layers, blks = lax.axis_size("layer"), lax.axis_size("blk")
    n = layers * blks
    ca, cr, lanes = source.shape
    count = temp_old.shape[0]
    cap = 2 * ca * cr // n
    stride = cap + 8
    whole, vmem = pl.BlockSpec(memory_space=pl.ANY), pl.BlockSpec(memory_space=pltpu.VMEM)

    def f32(*shape):
        return pltpu.VMEM(shape, jnp.float32)

    def i32(*shape):
        return pltpu.VMEM(shape, jnp.int32)

    field = f32(ca + 2 * WIDE, cr + 2 * ROWS, lanes)
    each = pltpu.SemaphoreType.DMA((n,))
    thermal = jax.ShapeDtypeStruct(temp_old.shape, jnp.float32)

    def exchange(*refs):
        exchange_kernel(layers, blks, *refs)

    inputs = [
        pltpu.with_memory_space_constraint(x, pltpu.HBM)
        for x in (source, sigma_ref, owner, slot, temp_old, heat_cap, conduct)
    ]
    potential = jax.ShapeDtypeStruct(source.shape, jnp.float32)
    row = jax.ShapeDtypeStruct((1, lanes), jnp.float32)
    results = pl.pallas_call(
        exchange,
        out_shape=(potential, thermal, row) + (thermal,) * 5,
        in_specs=[whole] * 7,
        out_specs=(vmem,) * 8,
        scratch_shapes=[
            f32(n * stride, lanes),
            i32(count // 32, 1, LANES), pltpu.SMEM((count // 32, 1, LANES), jnp.int32),
            i32(ca, cr), i32(ca, cr), f32(ca, cr, lanes),
            f32(count, lanes), f32(count, lanes), f32(count, lanes),
            i32(n, 1, LANES), i32(n, 1, LANES), i32(n, 1, LANES),
            i32(ca, 1, LANES), i32(n, 1, LANES),
            pltpu.SMEM((n, 1, LANES), jnp.int32),
            pltpu.SMEM((ca, 1, LANES), jnp.int32),
            pltpu.SMEM((n, 1, LANES), jnp.int32),
            f32(n * cap, lanes), f32(n * cap, lanes), f32(n * stride, lanes),
            field, field, field, field, field, field, field, field, field, field, field,
            f32(ca, cr, lanes), f32(ca * cr, lanes),
            pltpu.SemaphoreType.DMA((8,)),
            each, each, each, each, each, each,
            pltpu.SemaphoreType.DMA((2, 8)),
            pltpu.SemaphoreType.DMA((2, 8)),
        ],
        compiler_params=pltpu.CompilerParams(
            collective_id=0, has_side_effects=True, vmem_limit_bytes=40 << 20
        ),
    )(*inputs)

    def heat_step(*refs):
        thermal_kernel(float(source.size * n), *refs)

    return pl.pallas_call(
        heat_step,
        out_shape=(potential, thermal),
        in_specs=[whole] + [vmem] * 7,
        out_specs=(whole,) * 2,
        scratch_shapes=[f32(count, lanes), pltpu.SemaphoreType.DMA((5,))],
        compiler_params=pltpu.CompilerParams(vmem_limit_bytes=24 << 20),
    )(*results)


def solution(mesh):
    field = P("layer", "blk", None)
    index = P("layer", "blk")
    thermal = P(("blk", "layer"), None)
    return jax.shard_map(
        per_device,
        mesh=mesh,
        in_specs=(field, field, index, index, thermal, thermal, thermal),
        out_specs=(field, thermal),
        check_vma=False,
    )
```

```python
import jax
import jax.numpy as jnp
from jax import lax
from jax.experimental import pallas as pl
from jax.experimental.pallas import tpu as pltpu
from jax.sharding import PartitionSpec as P

JACOBI = 2
COUPLE = 0.4
THETA = 1.125
DELTA = 0.875

WIDE = 4
ROWS = 12
FROM = 8
EDGE = 4
LANES = 128
MESH = pl.DeviceIdType.MESH
DIRECTIONS = [(a, r) for r in (-1, 1, 0) for a in (-1, 1, 0) if (a, r) != (0, 0)]


def iota(shape, axis):
    return lax.broadcasted_iota(jnp.int32, shape, axis)


def ones(mask):
    return jnp.where(mask, 1.0, 0.0)


def dot(x, y, over):
    return lax.dot_general(
        x.astype(jnp.bfloat16), y.astype(jnp.bfloat16), (over, ((), ())),
        preferred_element_type=jnp.float32,
    )


def route(owner, slot, ask, places, blocks, cap):
    ca, cr = owner.shape
    n = ask.shape[0]
    earlier = ones(iota((cr, cr), 0) < iota((cr, cr), 1))
    seen = jnp.zeros((n, 1), jnp.float32)
    table = jnp.zeros((4 * n, LANES), jnp.float32)
    lane = iota((n, cr), 1).astype(jnp.float32)
    places[...] = jnp.zeros(places.shape, jnp.int32)
    for a in range(ca):
        name = owner[a : a + 1, :]
        mine = ones(iota((n, cr), 0) == name)
        before = dot(mine, earlier, ((1,), (0,))) + seen
        within = jnp.sum(mine * before, axis=0, keepdims=True).astype(jnp.int32)
        seen = seen + jnp.sum(mine, axis=1, keepdims=True)
        places[a, :, 0:cr] = jnp.clip(name * cap + within, 0, n * cap - 1)
        here = ones(iota((LANES, cr), 0) == within)
        code = slot[a : a + 1, :] + 1
        high = (code >> 5).astype(jnp.float32)
        low = (code & 31).astype(jnp.float32)
        digits = jnp.concatenate([mine * high, mine * low, mine * float(a), mine * lane], axis=0)
        table = table + dot(digits, here, ((1,), (1,)))
    codes = (table[0:n] * 32.0 + table[n : 2 * n]).astype(jnp.int32)
    block = (table[2 * n : 3 * n] * float(cr) + table[3 * n :]).astype(jnp.int32)
    for j in range(n):
        ask[j] = codes[j : j + 1]
        blocks[j] = jnp.clip(block[j : j + 1], 0, ca * cr - 1)


def invert(wanted, where_from, stride):
    n = wanted.shape[0]
    hn = where_from.shape[0]
    ln = 32

    def body(j, table):
        code = wanted[j] - 1
        at = ones(iota((hn, LANES), 0) == (code >> 5))
        low = ones(iota((ln, LANES), 0) == (code & 31))
        lane = iota((hn, LANES), 1).astype(jnp.float32)
        digits = jnp.concatenate([at * j.astype(jnp.float32), at * lane], axis=0)
        return table + dot(digits, low, ((1,), (1,)))

    table = lax.fori_loop(0, n, body, jnp.zeros((2 * hn, ln), jnp.float32), unroll=4)
    found = (table[:hn] * float(stride) + table[hn:]).astype(jnp.int32)
    found = jnp.clip(found, 0, n * stride - 1)
    where_from[...] = jnp.zeros(where_from.shape, jnp.int32)
    for h in range(hn):
        where_from[h, :, 0:ln] = found[h : h + 1]


def exchange_kernel(
    layers, blks,
    source, sigma_in, owner_in, slot_in, old_in, cap_in, conduct_in,
    potential, heat, sums, inv_d, base, first_t, left_n, right_n,
    arrived, where_v, where_from,
    owner, slot, sigma, temp_old, heat_cap, conduct,
    ask, wanted, wanted_at, places_v, blocks_v, asked, places, blocks,
    rows, fetched, out_rows,
    src, cond, brinks, inv, gr, gl, dir_a, wa, dir_b, wb, res, pot, temps, power,
    local_sem, ask_send, ask_recv, row_send, row_recv, pow_send, pow_recv,
    halo_send, halo_recv,
):
    n = layers * blks
    ca, cr, lanes = source.shape
    cap = fetched.shape[0] // n
    stride = cap + 8
    ext_r = cr + 2 * ROWS
    tall = cr + 2 * EDGE
    blk, layer = lax.axis_index("blk"), lax.axis_index("layer")
    me = blk * layers + layer

    def flips(x, size):
        out, bit = [x], 1
        while bit < size:
            by = bit - 2 * bit * lax.rem(lax.div(x, bit), 2)
            out += [value + by for value in out]
            bit *= 2
        return out

    def flip(x, mask, size):
        total, bit = 0, 1
        while bit < size:
            total = total + bit * lax.rem(lax.div(x, bit) + lax.div(mask, bit), 2)
            bit *= 2
        return total

    to_layers = flips(layer, layers)
    to_blks = flips(blk, blks)

    def others(body):
        for to_blk in to_blks[::-1]:
            for to_layer in to_layers[::-1]:
                if to_blk is not blk or to_layer is not layer:
                    body((to_blk, to_layer), to_blk * layers + to_layer)

    def others_long(body):
        def step(i, carry):
            k = jnp.where(lax.rem(i, 2) == 0, blks - 1 - lax.div(i, 2), blks // 2 - 1 - lax.div(i, 2))
            to_blk = flip(blk, k, blks)
            for to_layer in to_layers[::-1]:
                def go(to_layer=to_layer):
                    body((to_blk, to_layer), to_blk * layers + to_layer)

                if to_layer is layer:
                    pl.when(k > 0)(go)
                else:
                    go()
            return carry

        lax.fori_loop(0, blks, step, 0)

    barrier = pltpu.get_barrier_semaphore()
    others(lambda at, j: pl.semaphore_signal(barrier, inc=1, device_id=at, device_id_type=MESH))

    def local(src_ref, dst_ref, i):
        copy = pltpu.make_async_copy(src_ref, dst_ref, local_sem.at[i])
        copy.start()
        return copy

    get_owner = local(owner_in, owner, 0)
    get_slot = local(slot_in, slot, 1)
    get_src = local(source, src.at[pl.ds(WIDE, ca), pl.ds(ROWS, cr)], 2)
    get_old = local(old_in, temp_old, 3)
    get_sigma = local(sigma_in, sigma, 4)
    get_cap = local(cap_in, heat_cap, 5)
    get_conduct = local(conduct_in, conduct, 6)

    get_owner.wait()
    get_slot.wait()
    route(owner, slot, ask, places_v, blocks_v, cap)
    own_ask = local(ask.at[me], wanted.at[me], 0)
    set_places = local(places_v, places, 1)
    set_blocks = local(blocks_v, blocks, 7)
    get_src.wait()

    pl.semaphore_wait(barrier, n - 1)

    def remote(src_ref, dst_ref, send, recv, at):
        return pltpu.make_async_remote_copy(
            src_ref=src_ref, dst_ref=dst_ref, send_sem=send, recv_sem=recv,
            device_id=at, device_id_type=MESH,
        )

    def ask_copy(at, j, at_slot):
        return remote(ask.at[j], wanted.at[at_slot], ask_send.at[j], ask_recv.at[at_slot], at)

    others(lambda at, j: ask_copy(at, j, me).start())

    def halo(kind, d, field):
        step_a, step_r = DIRECTIONS[d]
        deep = 3 + kind if step_r == 0 else 2 + kind
        count_a = ca if step_a == 0 else deep
        count_r = cr if step_r == 0 else EDGE
        from_a = {0: WIDE, 1: WIDE + ca - deep, -1: WIDE}[step_a]
        to_a = {0: WIDE, 1: WIDE - deep, -1: WIDE + ca}[step_a]
        from_r = {0: ROWS, 1: ROWS + cr - EDGE, -1: ROWS}[step_r]
        to_r = {0: ROWS, 1: ROWS - EDGE, -1: ROWS + cr}[step_r]
        target = field.at[pl.ds(to_a, count_a), pl.ds(to_r, count_r)]
        if kind and step_r:
            target = brinks[0 if step_r > 0 else 1].at[pl.ds(to_a, count_a)]
        return remote(
            field.at[pl.ds(from_a, count_a), pl.ds(from_r, count_r)], target,
            halo_send.at[kind, d], halo_recv.at[kind, d],
            (lax.rem(blk + step_r + blks, blks), lax.rem(layer + step_a + layers, layers)),
        )

    def halo_all(kind, field, verb, chosen):
        for d in chosen:
            step_a = DIRECTIONS[d][0]
            if verb == "recv":
                step_a = -step_a

            def act(d=d):
                copy = halo(kind, d, field)
                {"start": copy.start, "recv": copy.wait_recv, "send": copy.wait_send}[verb]()

            if step_a == 0:
                act()
            else:
                pl.when(layer < layers - 1 if step_a > 0 else layer > 0)(act)

    every = range(len(DIRECTIONS))
    around_r = [d for d in every if DIRECTIONS[d][1] != 0]
    along_a = [d for d in every if DIRECTIONS[d][1] == 0]
    halo_all(0, src, "start", every)

    def clear(start):
        empty = jnp.zeros((WIDE, ext_r, lanes), jnp.float32)
        for field in (cond, dir_a, wa, dir_b, wb, pot):
            field[pl.ds(start, WIDE)] = empty
        for brink in brinks:
            brink[pl.ds(start, WIDE)] = jnp.zeros((WIDE, EDGE, lanes), jnp.float32)

    pl.when(layer == 0)(lambda: clear(0))
    pl.when(layer == layers - 1)(lambda: clear(WIDE + ca))

    own_ask.wait()
    others(lambda at, j: ask_copy(at, j, j).wait_recv())
    wanted_at[...] = jnp.clip(wanted[...] - 1, 0, temp_old.shape[0] - 1)
    local(wanted_at, asked, 0).wait()
    get_old.wait()

    def row_copy(at, j, at_slot):
        return remote(
            rows.at[pl.ds(pl.multiple_of(j * cap, 8), cap)],
            fetched.at[pl.ds(pl.multiple_of(at_slot * cap, 8), cap)],
            row_send.at[j], row_recv.at[at_slot], at,
        )

    def fill(target, start, table, j, origin):
        for c in range(cap):
            target[pl.ds(start + c, 1), :] = origin[pl.ds(table[j, 0, c], 1), :]

    def reply(at, j):
        fill(rows, pl.multiple_of(j * cap, 8), asked, j, temp_old)
        row_copy(at, j, me).start()

    others_long(reply)
    fill(fetched, pl.multiple_of(me * cap, 8), asked, me, temp_old)

    invert(wanted, where_v, stride)
    set_where = local(where_v, where_from, 0)
    get_cap.wait()
    get_conduct.wait()
    lane = iota((64, lanes), 1)

    def coefficients(b, carry):
        at = pl.ds(pl.multiple_of(b * 64, 8), 64)
        k = conduct[at, :]
        right = jnp.where(lane == lanes - 1, 0.0, 0.5 * (k + pltpu.roll(k, lanes - 1, 1)))
        left = jnp.where(lane == 0, 0.0, 0.5 * (k + pltpu.roll(k, 1, 1)))
        held = heat_cap[at, :]
        inverse = 1.0 / (held + left + right)
        old = temp_old[at, :]
        left = left * inverse
        right = right * inverse
        still = held * old * inverse
        inv_d[at, :] = inverse
        base[at, :] = still
        left_n[at, :] = left
        right_n[at, :] = right
        first_t[at, :] = still + left * pltpu.roll(old, 1, 1) + right * pltpu.roll(old, lanes - 1, 1)
        return carry

    lax.fori_loop(0, temp_old.shape[0] // 64, coefficients, 0)
    set_places.wait()
    set_blocks.wait()
    get_sigma.wait()

    others(lambda at, j: row_copy(at, j, j).wait_recv())

    def place(a, tiles):
        for t in tiles:
            for r in range(8 * t, 8 * t + 8):
                temps[a, r : r + 1, :] = fetched[pl.ds(places[a, 0, r], 1), :]
        for t in tiles:
            at = pl.ds(8 * t, 8)
            half = 0.5 * sigma[a, at, :] / (1.0 + COUPLE * temps[a, at, :])
            cond[WIDE + a, pl.ds(ROWS + 8 * t, 8), :] = half

    tiles = cr // 8

    def place_edges(a, carry):
        place(a, (0, tiles - 1))
        return carry

    def place_middle(a, carry):
        place(a, range(1, tiles - 1))
        return carry

    lax.fori_loop(0, ca, place_edges, 0, unroll=4)
    halo_all(1, cond, "start", around_r)
    lax.fori_loop(0, WIDE, place_middle, 0, unroll=2)
    lax.fori_loop(ca - WIDE, ca, place_middle, 0, unroll=2)
    halo_all(1, cond, "start", along_a)
    lax.fori_loop(WIDE, ca - WIDE, place_middle, 0, unroll=2)

    halo_all(0, src, "recv", every)
    halo_all(1, cond, "recv", along_a)

    ratio = THETA / DELTA
    rho = [1.0 / ratio]
    for _ in range(2):
        rho.append(1.0 / (2.0 * ratio - rho[-1]))

    def at_ends(height):
        lane = iota((height, lanes), 1)
        return lane == 0, lane == lanes - 1

    def next_l(x):
        return pltpu.roll(x, lanes - 1, 1)

    def back_l(x):
        return pltpu.roll(x, 1, 1)

    def solve_bands(starts, height, unroll):
        at_first, at_last = at_ends(height)

        def beside(field, e, r):
            up, down = field[e + 1, pl.ds(r, height), :], field[e - 1, pl.ds(r, height), :]
            return (up + down) + (field[e, pl.ds(r + 1, height), :] + field[e, pl.ds(r - 1, height), :])

        def sweep(body, reach):
            def slab(e, carry):
                for r in starts:
                    body(e, r)
                return carry

            lax.fori_loop(WIDE, WIDE + ca, slab, 0, unroll=unroll)

            @pl.when(layer > 0)
            def _():
                lax.fori_loop(WIDE - reach, WIDE, slab, 0, unroll=True)

            @pl.when(layer < layers - 1)
            def _():
                lax.fori_loop(WIDE + ca, WIDE + ca + reach, slab, 0, unroll=True)

        def first(e, r):
            at = pl.ds(r, height)
            here = cond[e, at, :]
            right = here + next_l(here)
            left = here + back_l(here)
            diag = (4.0 * here + beside(cond, e, r)) + (
                jnp.where(at_last, here, right) + jnp.where(at_first, here, left)
            )
            inverse = 1.0 / diag
            step = (inverse * src[e, at, :]) * (1.0 / THETA)
            gr[e, at, :] = jnp.where(at_last, 0.0, right)
            gl[e, at, :] = jnp.where(at_first, 0.0, left)
            inv[e, at, :] = inverse
            dir_a[e, at, :] = step
            wa[e, at, :] = here * step

        def pulls(field, weighted, e, r, v, here):
            at = pl.ds(r, height)
            sideways = gr[e, at, :] * next_l(v) + gl[e, at, :] * back_l(v)
            return (here * beside(field, e, r) + beside(weighted, e, r)) + sideways

        def second(e, r):
            at = pl.ds(r, height)
            v, here = dir_a[e, at, :], cond[e, at, :]
            rest = inv[e, at, :] * (src[e, at, :] + pulls(dir_a, wa, e, r, v, here)) - v
            step = (rho[1] * rho[0]) * v + (2.0 * rho[1] / DELTA) * rest
            res[e, at, :] = rest
            dir_b[e, at, :] = step
            wb[e, at, :] = here * step

        def third(e, r):
            at = pl.ds(r, height)
            v, here = dir_b[e, at, :], cond[e, at, :]
            rest = res[e, at, :] + inv[e, at, :] * pulls(dir_b, wb, e, r, v, here) - v
            step = (rho[2] * rho[1]) * v + (2.0 * rho[2] / DELTA) * rest
            pot[e, at, :] = dir_a[e, at, :] + v + step

        sweep(first, 3)
        sweep(second, 2)
        sweep(third, 1)

    def heat_bands(starts, height, skip, unroll, total):
        at_first, at_last = at_ends(height)

        def slab(a, total):
            e = a + WIDE
            for r in starts:
                def near(shift_e, shift_r):
                    return pot[e + shift_e, pl.ds(ROWS + r + shift_r, height), :]

                v = near(0, 0)
                gaps = [v - near(1, 0), v - near(-1, 0), v - near(0, 1), v - near(0, -1)]
                gaps.append(v - jnp.where(at_last, 0.0, next_l(v)))
                gaps.append(v - jnp.where(at_first, 0.0, back_l(v)))
                squares = [gap * gap for gap in gaps]
                result = (squares[0] + squares[1]) + (squares[2] + squares[3]) + (squares[4] + squares[5])
                result = cond[e, pl.ds(ROWS + r, height), :] * result
                power[pl.ds(pl.multiple_of(a * cr + r, 8), height), :] = result
                potential[a, r : r + height, :] = v
                kept = result[skip : height - skip]
                total = total + jnp.sum(kept.reshape(kept.shape[0] // 8, 8, lanes), axis=0)
            return total

        return lax.fori_loop(0, ca, slab, total, unroll=unroll)

    solve_bands((FROM,), tall, 8)
    total = heat_bands((0,), cr, 8, 8, jnp.zeros((8, lanes), jnp.float32))
    halo_all(1, cond, "recv", around_r)

    def bring(e, carry):
        cond[e, ROWS - EDGE : ROWS, :] = brinks[0][e]
        cond[e, ROWS + cr : ROWS + cr + EDGE, :] = brinks[1][e]
        return carry

    lax.fori_loop(0, ca + 2 * WIDE, bring, 0, unroll=8)
    solve_bands((FROM, FROM + tall - 8), 8, True)
    total = heat_bands((0, cr - 8), 8, 0, True, total)
    part = jnp.sum(total, axis=0, keepdims=True)

    def pow_copy(at, j, at_slot):
        return remote(
            out_rows.at[pl.ds(pl.multiple_of(j * stride, 8), cap + 1)],
            arrived.at[pl.ds(pl.multiple_of(at_slot * stride, 8), cap + 1)],
            pow_send.at[j], pow_recv.at[at_slot], at,
        )

    def send_power(at, j):
        start = pl.multiple_of(j * stride, 8)
        fill(out_rows, start, blocks, j, power)
        out_rows[pl.ds(start + cap, 1), :] = part
        pow_copy(at, j, me).start()

    others_long(send_power)
    start = pl.multiple_of(me * stride, 8)
    fill(arrived, start, blocks, me, power)
    arrived[pl.ds(start + cap, 1), :] = part

    halo_all(0, src, "send", every)
    halo_all(1, cond, "send", every)

    def sent(at, j):
        ask_copy(at, j, j).wait_send()
        row_copy(at, j, j).wait_send()
        pow_copy(at, j, j).wait_send()

    others(sent)
    set_where.wait()
    others(lambda at, j: pow_copy(at, j, j).wait_recv())

    def add(j, total):
        return total + arrived[pl.ds(j * stride + cap, 1), :]

    sums[...] = lax.fori_loop(0, n, add, jnp.zeros((1, lanes), jnp.float32), unroll=8)

    def gather(b, carry):
        for c in range(32):
            heat[pl.ds(b * 32 + c, 1), :] = arrived[pl.ds(where_from[b, 0, c], 1), :]
        return carry

    lax.fori_loop(0, where_from.shape[0], gather, 0, unroll=4)


def thermal_kernel(
    scale, potential_in, heat, sums, inv_d, base, first_t, left_n, right_n,
    potential, temp_out, temp_new, sem,
):
    through = pltpu.make_async_copy(potential_in, potential, sem.at[0])
    through.start()
    count, lanes = heat.shape
    factor = scale / jnp.sum(sums[...])
    step, pieces = 64, 4
    chunk = count // pieces

    def put(q):
        at = pl.ds(q * chunk, chunk)
        return pltpu.make_async_copy(temp_new.at[at], temp_out.at[at], sem.at[1 + q])

    def solve(b, carry):
        at = pl.ds(pl.multiple_of(b * step, 8), step)
        warm = heat[at, :] * factor * inv_d[at, :]
        current = first_t[at, :] + warm
        for _ in range(JACOBI - 1):
            before = pltpu.roll(current, 1, 1)
            after = pltpu.roll(current, lanes - 1, 1)
            current = (base[at, :] + warm) + left_n[at, :] * before + right_n[at, :] * after
        temp_new[at, :] = current
        return carry

    for q in range(pieces):
        lax.fori_loop(q * chunk // step, (q + 1) * chunk // step, solve, 0, unroll=True)
        put(q).start()
    for q in range(pieces):
        put(q).wait()
    through.wait()


def per_device(source, sigma_ref, owner, slot, temp_old, heat_cap, conduct):
    layers, blks = lax.axis_size("layer"), lax.axis_size("blk")
    n = layers * blks
    ca, cr, lanes = source.shape
    count = temp_old.shape[0]
    cap = 2 * ca * cr // n
    stride = cap + 8
    whole, vmem = pl.BlockSpec(memory_space=pl.ANY), pl.BlockSpec(memory_space=pltpu.VMEM)

    def f32(*shape):
        return pltpu.VMEM(shape, jnp.float32)

    def i32(*shape):
        return pltpu.VMEM(shape, jnp.int32)

    field = f32(ca + 2 * WIDE, cr + 2 * ROWS, lanes)
    each = pltpu.SemaphoreType.DMA((n,))
    thermal = jax.ShapeDtypeStruct(temp_old.shape, jnp.float32)

    def exchange(*refs):
        exchange_kernel(layers, blks, *refs)

    inputs = [
        pltpu.with_memory_space_constraint(x, pltpu.HBM)
        for x in (source, sigma_ref, owner, slot, temp_old, heat_cap, conduct)
    ]
    potential = jax.ShapeDtypeStruct(source.shape, jnp.float32)
    row = jax.ShapeDtypeStruct((1, lanes), jnp.float32)
    results = pl.pallas_call(
        exchange,
        out_shape=(potential, thermal, row) + (thermal,) * 5,
        in_specs=[whole] * 7,
        out_specs=(vmem,) * 8,
        scratch_shapes=[
            f32(n * stride, lanes),
            i32(count // 32, 1, LANES), pltpu.SMEM((count // 32, 1, LANES), jnp.int32),
            i32(ca, cr), i32(ca, cr), f32(ca, cr, lanes),
            f32(count, lanes), f32(count, lanes), f32(count, lanes),
            i32(n, 1, LANES), i32(n, 1, LANES), i32(n, 1, LANES),
            i32(ca, 1, LANES), i32(n, 1, LANES),
            pltpu.SMEM((n, 1, LANES), jnp.int32),
            pltpu.SMEM((ca, 1, LANES), jnp.int32),
            pltpu.SMEM((n, 1, LANES), jnp.int32),
            f32(n * cap, lanes), f32(n * cap, lanes), f32(n * stride, lanes),
            field, field, [f32(ca + 2 * WIDE, EDGE, lanes)] * 2,
            field, field, field, field, field, field, field, field, field,
            f32(ca, cr, lanes), f32(ca * cr, lanes),
            pltpu.SemaphoreType.DMA((8,)),
            each, each, each, each, each, each,
            pltpu.SemaphoreType.DMA((2, 8)),
            pltpu.SemaphoreType.DMA((2, 8)),
        ],
        compiler_params=pltpu.CompilerParams(
            collective_id=0, has_side_effects=True, vmem_limit_bytes=40 << 20
        ),
    )(*inputs)

    def heat_step(*refs):
        thermal_kernel(float(source.size * n), *refs)

    return pl.pallas_call(
        heat_step,
        out_shape=(potential, thermal),
        in_specs=[whole] + [vmem] * 7,
        out_specs=(whole,) * 2,
        scratch_shapes=[f32(count, lanes), pltpu.SemaphoreType.DMA((5,))],
        compiler_params=pltpu.CompilerParams(vmem_limit_bytes=24 << 20),
    )(*results)


def solution(mesh):
    field = P("layer", "blk", None)
    index = P("layer", "blk")
    thermal = P(("blk", "layer"), None)
    return jax.shard_map(
        per_device,
        mesh=mesh,
        in_specs=(field, field, index, index, thermal, thermal, thermal),
        out_specs=(field, thermal),
        check_vma=False,
    )
```

```python
import jax
import jax.numpy as jnp
from jax import lax
from jax.experimental import pallas as pl
from jax.experimental.pallas import tpu as pltpu
from jax.sharding import PartitionSpec as P

JACOBI = 2
COUPLE = 0.4
THETA = 1.125
DELTA = 0.875

WIDE = 4
ROWS = 12
FROM = 8
EDGE = 4
LANES = 128
MESH = pl.DeviceIdType.MESH
DIRECTIONS = [(a, r) for r in (-1, 1, 0) for a in (-1, 1, 0) if (a, r) != (0, 0)]


def iota(shape, axis):
    return lax.broadcasted_iota(jnp.int32, shape, axis)


def ones(mask):
    return jnp.where(mask, 1.0, 0.0)


def dot(x, y, over):
    return lax.dot_general(
        x.astype(jnp.bfloat16), y.astype(jnp.bfloat16), (over, ((), ())),
        preferred_element_type=jnp.float32,
    )


def route(owner, slot, ask, places, cap):
    ca, cr = owner.shape
    n = ask.shape[0]
    earlier = ones(iota((cr, cr), 0) < iota((cr, cr), 1))
    seen = jnp.zeros((n, 1), jnp.float32)
    table = jnp.zeros((2 * n, LANES), jnp.float32)
    places[...] = jnp.zeros(places.shape, jnp.int32)
    for a in range(ca):
        name = owner[a : a + 1, :]
        mine = ones(iota((n, cr), 0) == name)
        before = dot(mine, earlier, ((1,), (0,))) + seen
        within = jnp.sum(mine * before, axis=0, keepdims=True).astype(jnp.int32)
        seen = seen + jnp.sum(mine, axis=1, keepdims=True)
        places[a, :, 0:cr] = jnp.clip(name * cap + within, 0, n * cap - 1)
        here = ones(iota((LANES, cr), 0) == within)
        code = slot[a : a + 1, :] + 1
        high = (code >> 5).astype(jnp.float32)
        low = (code & 31).astype(jnp.float32)
        table = table + dot(jnp.concatenate([mine * high, mine * low], axis=0), here, ((1,), (1,)))
    codes = (table[0:n] * 32.0 + table[n:]).astype(jnp.int32)
    for j in range(n):
        ask[j] = codes[j : j + 1]


def list_blocks(owner, places, blocks, cap):
    ca, cr = owner.shape
    n = blocks.shape[0]
    table = jnp.zeros((2 * n, LANES), jnp.float32)
    lane = iota((n, cr), 1).astype(jnp.float32)
    for a in range(ca):
        name = owner[a : a + 1, :]
        mine = ones(iota((n, cr), 0) == name)
        here = ones(iota((LANES, cr), 0) == places[a, :, 0:cr] - name * cap)
        table = table + dot(jnp.concatenate([mine * float(a), mine * lane], axis=0), here, ((1,), (1,)))
    block = jnp.clip((table[0:n] * float(cr) + table[n:]).astype(jnp.int32), 0, ca * cr - 1)
    for j in range(n):
        blocks[j] = block[j : j + 1]


def invert(wanted, where_from, stride):
    n = wanted.shape[0]
    hn = where_from.shape[0]
    ln = 32

    def body(j, table):
        code = wanted[j] - 1
        at = ones(iota((hn, LANES), 0) == (code >> 5))
        low = ones(iota((ln, LANES), 0) == (code & 31))
        lane = iota((hn, LANES), 1).astype(jnp.float32)
        digits = jnp.concatenate([at * j.astype(jnp.float32), at * lane], axis=0)
        return table + dot(digits, low, ((1,), (1,)))

    table = lax.fori_loop(0, n, body, jnp.zeros((2 * hn, ln), jnp.float32), unroll=4)
    found = (table[:hn] * float(stride) + table[hn:]).astype(jnp.int32)
    found = jnp.clip(found, 0, n * stride - 1)
    where_from[...] = jnp.zeros(where_from.shape, jnp.int32)
    for h in range(hn):
        where_from[h, :, 0:ln] = found[h : h + 1]


def exchange_kernel(
    layers, blks,
    source, sigma_in, owner_in, slot_in, old_in, cap_in, conduct_in,
    potential, heat, sums, inv_d, base, first_t, left_n, right_n,
    arrived, where_v, where_from,
    owner, slot, sigma, temp_old, heat_cap, conduct,
    ask, wanted, wanted_at, places_v, blocks_v, asked, places, blocks,
    rows, fetched, out_rows,
    src, cond, brinks, inv, gr, gl, dir_a, wa, dir_b, wb, res, pot, temps, power,
    local_sem, ask_send, ask_recv, row_send, row_recv, pow_send, pow_recv,
    halo_send, halo_recv,
):
    n = layers * blks
    ca, cr, lanes = source.shape
    cap = fetched.shape[0] // n
    stride = cap + 8
    ext_r = cr + 2 * ROWS
    tall = cr + 2 * EDGE
    blk, layer = lax.axis_index("blk"), lax.axis_index("layer")
    me = blk * layers + layer

    def flips(x, size):
        out, bit = [x], 1
        while bit < size:
            by = bit - 2 * bit * lax.rem(lax.div(x, bit), 2)
            out += [value + by for value in out]
            bit *= 2
        return out

    def flip(x, mask, size):
        total, bit = 0, 1
        while bit < size:
            total = total + bit * lax.rem(lax.div(x, bit) + lax.div(mask, bit), 2)
            bit *= 2
        return total

    to_layers = flips(layer, layers)
    to_blks = flips(blk, blks)

    def others(body):
        for to_blk in to_blks[::-1]:
            for to_layer in to_layers[::-1]:
                if to_blk is not blk or to_layer is not layer:
                    body((to_blk, to_layer), to_blk * layers + to_layer)

    def others_long(body):
        def step(i, carry):
            k = jnp.where(lax.rem(i, 2) == 0, blks - 1 - lax.div(i, 2), blks // 2 - 1 - lax.div(i, 2))
            to_blk = flip(blk, k, blks)
            for to_layer in to_layers[::-1]:
                def go(to_layer=to_layer):
                    body((to_blk, to_layer), to_blk * layers + to_layer)

                if to_layer is layer:
                    pl.when(k > 0)(go)
                else:
                    go()
            return carry

        lax.fori_loop(0, blks, step, 0)

    barrier = pltpu.get_barrier_semaphore()
    others(lambda at, j: pl.semaphore_signal(barrier, inc=1, device_id=at, device_id_type=MESH))

    def local(src_ref, dst_ref, i):
        copy = pltpu.make_async_copy(src_ref, dst_ref, local_sem.at[i])
        copy.start()
        return copy

    get_owner = local(owner_in, owner, 0)
    get_slot = local(slot_in, slot, 1)
    get_src = local(source, src.at[pl.ds(WIDE, ca), pl.ds(ROWS, cr)], 2)
    get_old = local(old_in, temp_old, 3)
    get_sigma = local(sigma_in, sigma, 4)
    get_cap = local(cap_in, heat_cap, 5)
    get_conduct = local(conduct_in, conduct, 6)

    get_owner.wait()
    get_slot.wait()
    route(owner, slot, ask, places_v, cap)
    own_ask = local(ask.at[me], wanted.at[me], 0)
    set_places = local(places_v, places, 1)
    pl.semaphore_wait(barrier, n - 1)

    def remote(src_ref, dst_ref, send, recv, at):
        return pltpu.make_async_remote_copy(
            src_ref=src_ref, dst_ref=dst_ref, send_sem=send, recv_sem=recv,
            device_id=at, device_id_type=MESH,
        )

    def ask_copy(at, j, at_slot):
        return remote(ask.at[j], wanted.at[at_slot], ask_send.at[j], ask_recv.at[at_slot], at)

    others(lambda at, j: ask_copy(at, j, me).start())

    def halo(kind, d, field):
        step_a, step_r = DIRECTIONS[d]
        deep = 3 + kind if step_r == 0 else 2 + kind
        count_a = ca if step_a == 0 else deep
        count_r = cr if step_r == 0 else EDGE
        from_a = {0: WIDE, 1: WIDE + ca - deep, -1: WIDE}[step_a]
        to_a = {0: WIDE, 1: WIDE - deep, -1: WIDE + ca}[step_a]
        from_r = {0: ROWS, 1: ROWS + cr - EDGE, -1: ROWS}[step_r]
        to_r = {0: ROWS, 1: ROWS - EDGE, -1: ROWS + cr}[step_r]
        target = field.at[pl.ds(to_a, count_a), pl.ds(to_r, count_r)]
        if kind and step_r:
            target = brinks[0 if step_r > 0 else 1].at[pl.ds(to_a, count_a)]
        return remote(
            field.at[pl.ds(from_a, count_a), pl.ds(from_r, count_r)], target,
            halo_send.at[kind, d], halo_recv.at[kind, d],
            (lax.rem(blk + step_r + blks, blks), lax.rem(layer + step_a + layers, layers)),
        )

    def halo_all(kind, field, verb, chosen):
        for d in chosen:
            step_a = DIRECTIONS[d][0]
            if verb == "recv":
                step_a = -step_a

            def act(d=d):
                copy = halo(kind, d, field)
                {"start": copy.start, "recv": copy.wait_recv, "send": copy.wait_send}[verb]()

            if step_a == 0:
                act()
            else:
                pl.when(layer < layers - 1 if step_a > 0 else layer > 0)(act)

    every = range(len(DIRECTIONS))
    around_r = [d for d in every if DIRECTIONS[d][1] != 0]
    along_a = [d for d in every if DIRECTIONS[d][1] == 0]
    get_src.wait()
    halo_all(0, src, "start", every)

    def clear(start):
        empty = jnp.zeros((WIDE, ext_r, lanes), jnp.float32)
        for field in (cond, dir_a, wa, dir_b, wb, pot):
            field[pl.ds(start, WIDE)] = empty
        for brink in brinks:
            brink[pl.ds(start, WIDE)] = jnp.zeros((WIDE, EDGE, lanes), jnp.float32)

    pl.when(layer == 0)(lambda: clear(0))
    pl.when(layer == layers - 1)(lambda: clear(WIDE + ca))

    own_ask.wait()
    others(lambda at, j: ask_copy(at, j, j).wait_recv())
    wanted_at[...] = jnp.clip(wanted[...] - 1, 0, temp_old.shape[0] - 1)
    local(wanted_at, asked, 0).wait()
    get_old.wait()

    def row_copy(at, j, at_slot):
        return remote(
            rows.at[pl.ds(pl.multiple_of(j * cap, 8), cap)],
            fetched.at[pl.ds(pl.multiple_of(at_slot * cap, 8), cap)],
            row_send.at[j], row_recv.at[at_slot], at,
        )

    def fill(target, start, table, j, origin):
        for c in range(cap):
            target[pl.ds(start + c, 1), :] = origin[pl.ds(table[j, 0, c], 1), :]

    def reply(at, j):
        fill(rows, pl.multiple_of(j * cap, 8), asked, j, temp_old)
        row_copy(at, j, me).start()

    others_long(reply)
    fill(fetched, pl.multiple_of(me * cap, 8), asked, me, temp_old)

    list_blocks(owner, places_v, blocks_v, cap)
    set_blocks = local(blocks_v, blocks, 7)
    invert(wanted, where_v, stride)
    set_where = local(where_v, where_from, 0)
    get_cap.wait()
    get_conduct.wait()
    lane = iota((64, lanes), 1)

    def coefficients(b, carry):
        at = pl.ds(pl.multiple_of(b * 64, 8), 64)
        k = conduct[at, :]
        right = jnp.where(lane == lanes - 1, 0.0, 0.5 * (k + pltpu.roll(k, lanes - 1, 1)))
        left = jnp.where(lane == 0, 0.0, 0.5 * (k + pltpu.roll(k, 1, 1)))
        held = heat_cap[at, :]
        inverse = 1.0 / (held + left + right)
        old = temp_old[at, :]
        left = left * inverse
        right = right * inverse
        still = held * old * inverse
        inv_d[at, :] = inverse
        base[at, :] = still
        left_n[at, :] = left
        right_n[at, :] = right
        first_t[at, :] = still + left * pltpu.roll(old, 1, 1) + right * pltpu.roll(old, lanes - 1, 1)
        return carry

    lax.fori_loop(0, temp_old.shape[0] // 64, coefficients, 0)
    set_places.wait()
    set_blocks.wait()
    get_sigma.wait()

    others(lambda at, j: row_copy(at, j, j).wait_recv())

    def place(a, tiles):
        for t in tiles:
            for r in range(8 * t, 8 * t + 8):
                temps[a, r : r + 1, :] = fetched[pl.ds(places[a, 0, r], 1), :]
        for t in tiles:
            at = pl.ds(8 * t, 8)
            half = 0.5 * sigma[a, at, :] / (1.0 + COUPLE * temps[a, at, :])
            cond[WIDE + a, pl.ds(ROWS + 8 * t, 8), :] = half

    tiles = cr // 8

    def place_edges(a, carry):
        place(a, (0, tiles - 1))
        return carry

    def place_middle(a, carry):
        place(a, range(1, tiles - 1))
        return carry

    lax.fori_loop(0, ca, place_edges, 0, unroll=4)
    halo_all(1, cond, "start", around_r)
    lax.fori_loop(0, WIDE, place_middle, 0, unroll=2)
    lax.fori_loop(ca - WIDE, ca, place_middle, 0, unroll=2)
    halo_all(1, cond, "start", along_a)
    lax.fori_loop(WIDE, ca - WIDE, place_middle, 0, unroll=2)

    halo_all(0, src, "recv", every)
    halo_all(1, cond, "recv", along_a)

    ratio = THETA / DELTA
    rho = [1.0 / ratio]
    for _ in range(2):
        rho.append(1.0 / (2.0 * ratio - rho[-1]))

    def at_ends(height):
        lane = iota((height, lanes), 1)
        return lane == 0, lane == lanes - 1

    def next_l(x):
        return pltpu.roll(x, lanes - 1, 1)

    def back_l(x):
        return pltpu.roll(x, 1, 1)

    def solve_bands(starts, height, unroll):
        at_first, at_last = at_ends(height)

        def beside(field, e, r):
            up, down = field[e + 1, pl.ds(r, height), :], field[e - 1, pl.ds(r, height), :]
            return (up + down) + (field[e, pl.ds(r + 1, height), :] + field[e, pl.ds(r - 1, height), :])

        def sweep(body, reach):
            def slab(e, carry):
                for r in starts:
                    body(e, r)
                return carry

            lax.fori_loop(WIDE, WIDE + ca, slab, 0, unroll=unroll)

            @pl.when(layer > 0)
            def _():
                lax.fori_loop(WIDE - reach, WIDE, slab, 0, unroll=True)

            @pl.when(layer < layers - 1)
            def _():
                lax.fori_loop(WIDE + ca, WIDE + ca + reach, slab, 0, unroll=True)

        def first(e, r):
            at = pl.ds(r, height)
            here = cond[e, at, :]
            right = here + next_l(here)
            left = here + back_l(here)
            diag = (4.0 * here + beside(cond, e, r)) + (
                jnp.where(at_last, here, right) + jnp.where(at_first, here, left)
            )
            inverse = 1.0 / diag
            step = (inverse * src[e, at, :]) * (1.0 / THETA)
            gr[e, at, :] = jnp.where(at_last, 0.0, right)
            gl[e, at, :] = jnp.where(at_first, 0.0, left)
            inv[e, at, :] = inverse
            dir_a[e, at, :] = step
            wa[e, at, :] = here * step

        def pulls(field, weighted, e, r, v, here):
            at = pl.ds(r, height)
            sideways = gr[e, at, :] * next_l(v) + gl[e, at, :] * back_l(v)
            return (here * beside(field, e, r) + beside(weighted, e, r)) + sideways

        def second(e, r):
            at = pl.ds(r, height)
            v, here = dir_a[e, at, :], cond[e, at, :]
            rest = inv[e, at, :] * (src[e, at, :] + pulls(dir_a, wa, e, r, v, here)) - v
            step = (rho[1] * rho[0]) * v + (2.0 * rho[1] / DELTA) * rest
            res[e, at, :] = rest
            dir_b[e, at, :] = step
            wb[e, at, :] = here * step

        def third(e, r):
            at = pl.ds(r, height)
            v, here = dir_b[e, at, :], cond[e, at, :]
            rest = res[e, at, :] + inv[e, at, :] * pulls(dir_b, wb, e, r, v, here) - v
            step = (rho[2] * rho[1]) * v + (2.0 * rho[2] / DELTA) * rest
            pot[e, at, :] = dir_a[e, at, :] + v + step

        sweep(first, 3)
        sweep(second, 2)
        sweep(third, 1)

    def heat_bands(starts, height, skip, unroll, total):
        at_first, at_last = at_ends(height)

        def slab(a, total):
            e = a + WIDE
            for r in starts:
                def near(shift_e, shift_r):
                    return pot[e + shift_e, pl.ds(ROWS + r + shift_r, height), :]

                v = near(0, 0)
                gaps = [v - near(1, 0), v - near(-1, 0), v - near(0, 1), v - near(0, -1)]
                gaps.append(v - jnp.where(at_last, 0.0, next_l(v)))
                gaps.append(v - jnp.where(at_first, 0.0, back_l(v)))
                squares = [gap * gap for gap in gaps]
                result = (squares[0] + squares[1]) + (squares[2] + squares[3]) + (squares[4] + squares[5])
                result = cond[e, pl.ds(ROWS + r, height), :] * result
                power[pl.ds(pl.multiple_of(a * cr + r, 8), height), :] = result
                potential[a, r : r + height, :] = v
                kept = result[skip : height - skip]
                total = total + jnp.sum(kept.reshape(kept.shape[0] // 8, 8, lanes), axis=0)
            return total

        return lax.fori_loop(0, ca, slab, total, unroll=unroll)

    solve_bands((FROM,), tall, 8)
    total = heat_bands((0,), cr, 8, 8, jnp.zeros((8, lanes), jnp.float32))
    halo_all(1, cond, "recv", around_r)

    def bring(e, carry):
        cond[e, ROWS - EDGE : ROWS, :] = brinks[0][e]
        cond[e, ROWS + cr : ROWS + cr + EDGE, :] = brinks[1][e]
        return carry

    lax.fori_loop(0, ca + 2 * WIDE, bring, 0, unroll=8)
    solve_bands((FROM, FROM + tall - 8), 8, True)
    total = heat_bands((0, cr - 8), 8, 0, True, total)
    part = jnp.sum(total, axis=0, keepdims=True)

    def pow_copy(at, j, at_slot):
        return remote(
            out_rows.at[pl.ds(pl.multiple_of(j * stride, 8), cap + 1)],
            arrived.at[pl.ds(pl.multiple_of(at_slot * stride, 8), cap + 1)],
            pow_send.at[j], pow_recv.at[at_slot], at,
        )

    def send_power(at, j):
        start = pl.multiple_of(j * stride, 8)
        fill(out_rows, start, blocks, j, power)
        out_rows[pl.ds(start + cap, 1), :] = part
        pow_copy(at, j, me).start()

    others_long(send_power)
    start = pl.multiple_of(me * stride, 8)
    fill(arrived, start, blocks, me, power)
    arrived[pl.ds(start + cap, 1), :] = part

    halo_all(0, src, "send", every)
    halo_all(1, cond, "send", every)

    def sent(at, j):
        ask_copy(at, j, j).wait_send()
        row_copy(at, j, j).wait_send()
        pow_copy(at, j, j).wait_send()

    others(sent)
    set_where.wait()
    others(lambda at, j: pow_copy(at, j, j).wait_recv())

    def add(j, total):
        return total + arrived[pl.ds(j * stride + cap, 1), :]

    sums[...] = lax.fori_loop(0, n, add, jnp.zeros((1, lanes), jnp.float32), unroll=8)

    def gather(b, carry):
        for c in range(32):
            heat[pl.ds(b * 32 + c, 1), :] = arrived[pl.ds(where_from[b, 0, c], 1), :]
        return carry

    lax.fori_loop(0, where_from.shape[0], gather, 0, unroll=4)


def thermal_kernel(
    scale, potential_in, heat, sums, inv_d, base, first_t, left_n, right_n,
    potential, temp_out, temp_new, sem,
):
    through = pltpu.make_async_copy(potential_in, potential, sem.at[0])
    through.start()
    count, lanes = heat.shape
    factor = scale / jnp.sum(sums[...])
    step, pieces = 64, 4
    chunk = count // pieces

    def put(q):
        at = pl.ds(q * chunk, chunk)
        return pltpu.make_async_copy(temp_new.at[at], temp_out.at[at], sem.at[1 + q])

    def solve(b, carry):
        at = pl.ds(pl.multiple_of(b * step, 8), step)
        warm = heat[at, :] * factor * inv_d[at, :]
        current = first_t[at, :] + warm
        for _ in range(JACOBI - 1):
            before = pltpu.roll(current, 1, 1)
            after = pltpu.roll(current, lanes - 1, 1)
            current = (base[at, :] + warm) + left_n[at, :] * before + right_n[at, :] * after
        temp_new[at, :] = current
        return carry

    for q in range(pieces):
        lax.fori_loop(q * chunk // step, (q + 1) * chunk // step, solve, 0, unroll=True)
        put(q).start()
    for q in range(pieces):
        put(q).wait()
    through.wait()


def per_device(source, sigma_ref, owner, slot, temp_old, heat_cap, conduct):
    layers, blks = lax.axis_size("layer"), lax.axis_size("blk")
    n = layers * blks
    ca, cr, lanes = source.shape
    count = temp_old.shape[0]
    cap = 2 * ca * cr // n
    stride = cap + 8
    whole, vmem = pl.BlockSpec(memory_space=pl.ANY), pl.BlockSpec(memory_space=pltpu.VMEM)

    def f32(*shape):
        return pltpu.VMEM(shape, jnp.float32)

    def i32(*shape):
        return pltpu.VMEM(shape, jnp.int32)

    field = f32(ca + 2 * WIDE, cr + 2 * ROWS, lanes)
    each = pltpu.SemaphoreType.DMA((n,))
    thermal = jax.ShapeDtypeStruct(temp_old.shape, jnp.float32)

    def exchange(*refs):
        exchange_kernel(layers, blks, *refs)

    inputs = [
        pltpu.with_memory_space_constraint(x, pltpu.HBM)
        for x in (source, sigma_ref, owner, slot, temp_old, heat_cap, conduct)
    ]
    potential = jax.ShapeDtypeStruct(source.shape, jnp.float32)
    row = jax.ShapeDtypeStruct((1, lanes), jnp.float32)
    results = pl.pallas_call(
        exchange,
        out_shape=(potential, thermal, row) + (thermal,) * 5,
        in_specs=[whole] * 7,
        out_specs=(vmem,) * 8,
        scratch_shapes=[
            f32(n * stride, lanes),
            i32(count // 32, 1, LANES), pltpu.SMEM((count // 32, 1, LANES), jnp.int32),
            i32(ca, cr), i32(ca, cr), f32(ca, cr, lanes),
            f32(count, lanes), f32(count, lanes), f32(count, lanes),
            i32(n, 1, LANES), i32(n, 1, LANES), i32(n, 1, LANES),
            i32(ca, 1, LANES), i32(n, 1, LANES),
            pltpu.SMEM((n, 1, LANES), jnp.int32),
            pltpu.SMEM((ca, 1, LANES), jnp.int32),
            pltpu.SMEM((n, 1, LANES), jnp.int32),
            f32(n * cap, lanes), f32(n * cap, lanes), f32(n * stride, lanes),
            field, field, [f32(ca + 2 * WIDE, EDGE, lanes)] * 2,
            field, field, field, field, field, field, field, field, field,
            f32(ca, cr, lanes), f32(ca * cr, lanes),
            pltpu.SemaphoreType.DMA((8,)),
            each, each, each, each, each, each,
            pltpu.SemaphoreType.DMA((2, 8)),
            pltpu.SemaphoreType.DMA((2, 8)),
        ],
        compiler_params=pltpu.CompilerParams(
            collective_id=0, has_side_effects=True, vmem_limit_bytes=40 << 20
        ),
    )(*inputs)

    def heat_step(*refs):
        thermal_kernel(float(source.size * n), *refs)

    return pl.pallas_call(
        heat_step,
        out_shape=(potential, thermal),
        in_specs=[whole] + [vmem] * 7,
        out_specs=(whole,) * 2,
        scratch_shapes=[f32(count, lanes), pltpu.SemaphoreType.DMA((5,))],
        compiler_params=pltpu.CompilerParams(vmem_limit_bytes=24 << 20),
    )(*results)


def solution(mesh):
    field = P("layer", "blk", None)
    index = P("layer", "blk")
    thermal = P(("blk", "layer"), None)
    return jax.shard_map(
        per_device,
        mesh=mesh,
        in_specs=(field, field, index, index, thermal, thermal, thermal),
        out_specs=(field, thermal),
        check_vma=False,
    )
```

```python
import jax
import jax.numpy as jnp
from jax import lax
from jax.experimental import pallas as pl
from jax.experimental.pallas import tpu as pltpu
from jax.sharding import PartitionSpec as P

JACOBI = 2
COUPLE = 0.4
THETA = 1.125
DELTA = 0.875

WIDE = 4
ROWS = 12
FROM = 8
EDGE = 4
LANES = 128
MESH = pl.DeviceIdType.MESH
DIRECTIONS = [(a, r) for a in (0, -1, 1) for r in (-1, 1, 0) if (a, r) != (0, 0)]


def iota(shape, axis):
    return lax.broadcasted_iota(jnp.int32, shape, axis)


def ones(mask):
    return jnp.where(mask, 1.0, 0.0)


def dot(x, y, over):
    return lax.dot_general(
        x.astype(jnp.bfloat16), y.astype(jnp.bfloat16), (over, ((), ())),
        preferred_element_type=jnp.float32,
    )


def route(owner, slot, ask, places, cap):
    ca, cr = owner.shape
    n = ask.shape[0]
    earlier = ones(iota((cr, cr), 0) < iota((cr, cr), 1))
    seen = jnp.zeros((n, 1), jnp.float32)
    table = jnp.zeros((2 * n, LANES), jnp.float32)
    places[...] = jnp.zeros(places.shape, jnp.int32)
    for a in range(ca):
        name = owner[a : a + 1, :]
        mine = ones(iota((n, cr), 0) == name)
        before = dot(mine, earlier, ((1,), (0,))) + seen
        within = jnp.sum(mine * before, axis=0, keepdims=True).astype(jnp.int32)
        seen = seen + jnp.sum(mine, axis=1, keepdims=True)
        places[a, :, 0:cr] = jnp.clip(name * cap + within, 0, n * cap - 1)
        here = ones(iota((LANES, cr), 0) == within)
        code = slot[a : a + 1, :] + 1
        high = (code >> 5).astype(jnp.float32)
        low = (code & 31).astype(jnp.float32)
        table = table + dot(jnp.concatenate([mine * high, mine * low], axis=0), here, ((1,), (1,)))
    codes = (table[0:n] * 32.0 + table[n:]).astype(jnp.int32)
    for j in range(n):
        ask[j] = codes[j : j + 1]


def list_blocks(owner, places, blocks, cap):
    ca, cr = owner.shape
    n = blocks.shape[0]
    table = jnp.zeros((2 * n, LANES), jnp.float32)
    lane = iota((n, cr), 1).astype(jnp.float32)
    for a in range(ca):
        name = owner[a : a + 1, :]
        mine = ones(iota((n, cr), 0) == name)
        here = ones(iota((LANES, cr), 0) == places[a, :, 0:cr] - name * cap)
        table = table + dot(jnp.concatenate([mine * float(a), mine * lane], axis=0), here, ((1,), (1,)))
    block = jnp.clip((table[0:n] * float(cr) + table[n:]).astype(jnp.int32), 0, ca * cr - 1)
    for j in range(n):
        blocks[j] = block[j : j + 1]


def invert(wanted, where_from, stride):
    n = wanted.shape[0]
    hn = where_from.shape[0]
    ln = 32

    def body(j, table):
        code = wanted[j] - 1
        at = ones(iota((hn, LANES), 0) == (code >> 5))
        low = ones(iota((ln, LANES), 0) == (code & 31))
        lane = iota((hn, LANES), 1).astype(jnp.float32)
        digits = jnp.concatenate([at * j.astype(jnp.float32), at * lane], axis=0)
        return table + dot(digits, low, ((1,), (1,)))

    table = lax.fori_loop(0, n, body, jnp.zeros((2 * hn, ln), jnp.float32), unroll=4)
    found = (table[:hn] * float(stride) + table[hn:]).astype(jnp.int32)
    found = jnp.clip(found, 0, n * stride - 1)
    where_from[...] = jnp.zeros(where_from.shape, jnp.int32)
    for h in range(hn):
        where_from[h, :, 0:ln] = found[h : h + 1]


def exchange_kernel(
    layers, blks,
    source, sigma_in, owner_in, slot_in, old_in, cap_in, conduct_in,
    potential, heat, sums, inv_d, base, first_t, left_n, right_n,
    arrived, where_v, where_from,
    owner, slot, sigma, temp_old, heat_cap, conduct,
    ask, wanted, wanted_at, places_v, blocks_v, asked, places, blocks,
    rows, fetched, out_rows,
    src, cond, brinks, inv, gr, gl, dir_a, wa, dir_b, wb, res, pot, temps, power,
    local_sem, ask_send, ask_recv, row_send, row_recv, pow_send, pow_recv,
    halo_send, halo_recv,
):
    n = layers * blks
    ca, cr, lanes = source.shape
    cap = fetched.shape[0] // n
    stride = cap + 8
    ext_r = cr + 2 * ROWS
    tall = cr + 2 * EDGE
    blk, layer = lax.axis_index("blk"), lax.axis_index("layer")
    me = blk * layers + layer

    def flips(x, size):
        out, bit = [x], 1
        while bit < size:
            by = bit - 2 * bit * lax.rem(lax.div(x, bit), 2)
            out += [value + by for value in out]
            bit *= 2
        return out

    def flip(x, mask, size):
        total, bit = 0, 1
        while bit < size:
            total = total + bit * lax.rem(lax.div(x, bit) + lax.div(mask, bit), 2)
            bit *= 2
        return total

    to_layers = flips(layer, layers)
    to_blks = flips(blk, blks)

    def others(body):
        for to_blk in to_blks[::-1]:
            for to_layer in to_layers[::-1]:
                if to_blk is not blk or to_layer is not layer:
                    body((to_blk, to_layer), to_blk * layers + to_layer)

    def others_long(body):
        def step(i, carry):
            k = jnp.where(lax.rem(i, 2) == 0, blks - 1 - lax.div(i, 2), blks // 2 - 1 - lax.div(i, 2))
            to_blk = flip(blk, k, blks)
            for to_layer in to_layers[::-1]:
                def go(to_layer=to_layer):
                    body((to_blk, to_layer), to_blk * layers + to_layer)

                if to_layer is layer:
                    pl.when(k > 0)(go)
                else:
                    go()
            return carry

        lax.fori_loop(0, blks, step, 0)

    barrier = pltpu.get_barrier_semaphore()
    others(lambda at, j: pl.semaphore_signal(barrier, inc=1, device_id=at, device_id_type=MESH))

    def local(src_ref, dst_ref, i):
        copy = pltpu.make_async_copy(src_ref, dst_ref, local_sem.at[i])
        copy.start()
        return copy

    get_owner = local(owner_in, owner, 0)
    get_slot = local(slot_in, slot, 1)
    get_src = local(source, src.at[pl.ds(WIDE, ca), pl.ds(ROWS, cr)], 2)
    get_old = local(old_in, temp_old, 3)
    get_sigma = local(sigma_in, sigma, 4)
    get_cap = local(cap_in, heat_cap, 5)
    get_conduct = local(conduct_in, conduct, 6)

    get_owner.wait()
    get_slot.wait()
    route(owner, slot, ask, places_v, cap)
    own_ask = local(ask.at[me], wanted.at[me], 0)
    set_places = local(places_v, places, 1)
    pl.semaphore_wait(barrier, n - 1)

    def remote(src_ref, dst_ref, send, recv, at):
        return pltpu.make_async_remote_copy(
            src_ref=src_ref, dst_ref=dst_ref, send_sem=send, recv_sem=recv,
            device_id=at, device_id_type=MESH,
        )

    def ask_copy(at, j, at_slot):
        return remote(ask.at[j], wanted.at[at_slot], ask_send.at[j], ask_recv.at[at_slot], at)

    others(lambda at, j: ask_copy(at, j, me).start())

    def halo(kind, d, field):
        step_a, step_r = DIRECTIONS[d]
        deep = 3 + kind if step_r == 0 else 2 + kind
        count_a = ca if step_a == 0 else deep
        count_r = cr if step_r == 0 else EDGE
        from_a = {0: WIDE, 1: WIDE + ca - deep, -1: WIDE}[step_a]
        to_a = {0: WIDE, 1: WIDE - deep, -1: WIDE + ca}[step_a]
        from_r = {0: ROWS, 1: ROWS + cr - EDGE, -1: ROWS}[step_r]
        to_r = {0: ROWS, 1: ROWS - EDGE, -1: ROWS + cr}[step_r]
        target = field.at[pl.ds(to_a, count_a), pl.ds(to_r, count_r)]
        if kind and step_r:
            target = brinks[0 if step_r > 0 else 1].at[pl.ds(to_a, count_a)]
        return remote(
            field.at[pl.ds(from_a, count_a), pl.ds(from_r, count_r)], target,
            halo_send.at[kind, d], halo_recv.at[kind, d],
            (lax.rem(blk + step_r + blks, blks), lax.rem(layer + step_a + layers, layers)),
        )

    def halo_all(kind, field, verb, chosen):
        for d in chosen:
            step_a = DIRECTIONS[d][0]
            if verb == "recv":
                step_a = -step_a

            def act(d=d):
                copy = halo(kind, d, field)
                {"start": copy.start, "recv": copy.wait_recv, "send": copy.wait_send}[verb]()

            if step_a == 0:
                act()
            else:
                pl.when(layer < layers - 1 if step_a > 0 else layer > 0)(act)

    every = range(len(DIRECTIONS))
    around_r = [d for d in every if DIRECTIONS[d][1] != 0]
    along_a = [d for d in every if DIRECTIONS[d][1] == 0]
    get_src.wait()
    halo_all(0, src, "start", every)

    def clear(start):
        empty = jnp.zeros((WIDE, ext_r, lanes), jnp.float32)
        for field in (cond, dir_a, wa, dir_b, wb, pot):
            field[pl.ds(start, WIDE)] = empty
        for brink in brinks:
            brink[pl.ds(start, WIDE)] = jnp.zeros((WIDE, EDGE, lanes), jnp.float32)

    pl.when(layer == 0)(lambda: clear(0))
    pl.when(layer == layers - 1)(lambda: clear(WIDE + ca))

    own_ask.wait()
    others(lambda at, j: ask_copy(at, j, j).wait_recv())
    wanted_at[...] = jnp.clip(wanted[...] - 1, 0, temp_old.shape[0] - 1)
    local(wanted_at, asked, 0).wait()
    get_old.wait()

    def row_copy(at, j, at_slot):
        return remote(
            rows.at[pl.ds(pl.multiple_of(j * cap, 8), cap)],
            fetched.at[pl.ds(pl.multiple_of(at_slot * cap, 8), cap)],
            row_send.at[j], row_recv.at[at_slot], at,
        )

    def fill(target, start, table, j, origin):
        for c in range(cap):
            target[pl.ds(start + c, 1), :] = origin[pl.ds(table[j, 0, c], 1), :]

    def reply(at, j):
        fill(rows, pl.multiple_of(j * cap, 8), asked, j, temp_old)
        row_copy(at, j, me).start()

    others_long(reply)
    fill(fetched, pl.multiple_of(me * cap, 8), asked, me, temp_old)

    list_blocks(owner, places_v, blocks_v, cap)
    set_blocks = local(blocks_v, blocks, 7)
    invert(wanted, where_v, stride)
    set_where = local(where_v, where_from, 0)
    get_cap.wait()
    get_conduct.wait()
    lane = iota((64, lanes), 1)

    def coefficients(b, carry):
        at = pl.ds(pl.multiple_of(b * 64, 8), 64)
        k = conduct[at, :]
        right = jnp.where(lane == lanes - 1, 0.0, 0.5 * (k + pltpu.roll(k, lanes - 1, 1)))
        left = jnp.where(lane == 0, 0.0, 0.5 * (k + pltpu.roll(k, 1, 1)))
        held = heat_cap[at, :]
        inverse = 1.0 / (held + left + right)
        old = temp_old[at, :]
        left = left * inverse
        right = right * inverse
        still = held * old * inverse
        inv_d[at, :] = inverse
        base[at, :] = still
        left_n[at, :] = left
        right_n[at, :] = right
        first_t[at, :] = still + left * pltpu.roll(old, 1, 1) + right * pltpu.roll(old, lanes - 1, 1)
        return carry

    lax.fori_loop(0, temp_old.shape[0] // 64, coefficients, 0)
    set_places.wait()
    set_blocks.wait()
    get_sigma.wait()

    others(lambda at, j: row_copy(at, j, j).wait_recv())

    def place(a, spans):
        for start, height in spans:
            for r in range(start, start + height):
                temps[a, r : r + 1, :] = fetched[pl.ds(places[a, 0, r], 1), :]
        for start, height in spans:
            at = pl.ds(start, height)
            half = 0.5 * sigma[a, at, :] / (1.0 + COUPLE * temps[a, at, :])
            cond[WIDE + a, pl.ds(ROWS + start, height), :] = half

    def place_edges(a, carry):
        place(a, ((0, EDGE), (cr - EDGE, EDGE)))
        return carry

    def place_middle(a, carry):
        inner = [(r, 8) for r in range(8, cr - 8, 8)]
        place(a, [(EDGE, 8 - EDGE), *inner, (cr - 8, 8 - EDGE)])
        return carry

    lax.fori_loop(0, ca, place_edges, 0, unroll=4)
    halo_all(1, cond, "start", around_r)
    lax.fori_loop(0, WIDE, place_middle, 0, unroll=2)
    lax.fori_loop(ca - WIDE, ca, place_middle, 0, unroll=2)
    halo_all(1, cond, "start", along_a)
    lax.fori_loop(WIDE, ca - WIDE, place_middle, 0, unroll=2)

    halo_all(0, src, "recv", every)
    halo_all(1, cond, "recv", along_a)

    ratio = THETA / DELTA
    rho = [1.0 / ratio]
    for _ in range(2):
        rho.append(1.0 / (2.0 * ratio - rho[-1]))

    def at_ends(height):
        lane = iota((height, lanes), 1)
        return lane == 0, lane == lanes - 1

    def next_l(x):
        return pltpu.roll(x, lanes - 1, 1)

    def back_l(x):
        return pltpu.roll(x, 1, 1)

    def solve_bands(starts, height, unroll):
        at_first, at_last = at_ends(height)

        def beside(field, e, r):
            up, down = field[e + 1, pl.ds(r, height), :], field[e - 1, pl.ds(r, height), :]
            return (up + down) + (field[e, pl.ds(r + 1, height), :] + field[e, pl.ds(r - 1, height), :])

        def sweep(body, reach):
            def slab(e, carry):
                for r in starts:
                    body(e, r)
                return carry

            if unroll is True:
                lax.fori_loop(WIDE - reach, WIDE + ca + reach, slab, 0, unroll=True)
                return
            lax.fori_loop(WIDE, WIDE + ca, slab, 0, unroll=unroll)

            @pl.when(layer > 0)
            def _():
                lax.fori_loop(WIDE - reach, WIDE, slab, 0, unroll=True)

            @pl.when(layer < layers - 1)
            def _():
                lax.fori_loop(WIDE + ca, WIDE + ca + reach, slab, 0, unroll=True)

        def held(e, step):
            if unroll is not True:
                return step
            at = layer * ca + e - WIDE
            return jnp.where(jnp.logical_and(at >= 0, at < layers * ca), step, 0.0)

        def first(e, r):
            at = pl.ds(r, height)
            here = cond[e, at, :]
            right = here + next_l(here)
            left = here + back_l(here)
            diag = (4.0 * here + beside(cond, e, r)) + (
                jnp.where(at_last, here, right) + jnp.where(at_first, here, left)
            )
            inverse = 1.0 / diag
            step = held(e, (inverse * src[e, at, :]) * (1.0 / THETA))
            gr[e, at, :] = jnp.where(at_last, 0.0, right)
            gl[e, at, :] = jnp.where(at_first, 0.0, left)
            inv[e, at, :] = inverse
            dir_a[e, at, :] = step
            wa[e, at, :] = here * step

        def pulls(field, weighted, e, r, v, here):
            at = pl.ds(r, height)
            sideways = gr[e, at, :] * next_l(v) + gl[e, at, :] * back_l(v)
            return (here * beside(field, e, r) + beside(weighted, e, r)) + sideways

        def second(e, r):
            at = pl.ds(r, height)
            v, here = dir_a[e, at, :], cond[e, at, :]
            rest = inv[e, at, :] * (src[e, at, :] + pulls(dir_a, wa, e, r, v, here)) - v
            step = held(e, (rho[1] * rho[0]) * v + (2.0 * rho[1] / DELTA) * rest)
            res[e, at, :] = rest
            dir_b[e, at, :] = step
            wb[e, at, :] = here * step

        def third(e, r):
            at = pl.ds(r, height)
            v, here = dir_b[e, at, :], cond[e, at, :]
            rest = res[e, at, :] + inv[e, at, :] * pulls(dir_b, wb, e, r, v, here) - v
            step = held(e, (rho[2] * rho[1]) * v + (2.0 * rho[2] / DELTA) * rest)
            pot[e, at, :] = dir_a[e, at, :] + v + step

        sweep(first, 3)
        sweep(second, 2)
        sweep(third, 1)

    def heat_bands(starts, height, skip, unroll, total):
        at_first, at_last = at_ends(height)

        def slab(a, total):
            e = a + WIDE
            for r in starts:
                def near(shift_e, shift_r):
                    return pot[e + shift_e, pl.ds(ROWS + r + shift_r, height), :]

                v = near(0, 0)
                gaps = [v - near(1, 0), v - near(-1, 0), v - near(0, 1), v - near(0, -1)]
                gaps.append(v - jnp.where(at_last, 0.0, next_l(v)))
                gaps.append(v - jnp.where(at_first, 0.0, back_l(v)))
                squares = [gap * gap for gap in gaps]
                result = (squares[0] + squares[1]) + (squares[2] + squares[3]) + (squares[4] + squares[5])
                result = cond[e, pl.ds(ROWS + r, height), :] * result
                power[pl.ds(pl.multiple_of(a * cr + r, 8), height), :] = result
                potential[a, r : r + height, :] = v
                kept = result[skip : height - skip]
                total = total + jnp.sum(kept.reshape(kept.shape[0] // 8, 8, lanes), axis=0)
            return total

        return lax.fori_loop(0, ca, slab, total, unroll=unroll)

    solve_bands((FROM,), tall, 8)
    total = heat_bands((0,), cr, 8, 8, jnp.zeros((8, lanes), jnp.float32))
    halo_all(1, cond, "recv", around_r)

    def bring(e, carry):
        cond[e, ROWS - EDGE : ROWS, :] = brinks[0][e]
        cond[e, ROWS + cr : ROWS + cr + EDGE, :] = brinks[1][e]
        return carry

    lax.fori_loop(0, ca + 2 * WIDE, bring, 0, unroll=8)
    solve_bands((FROM, FROM + tall - 8), 8, True)
    total = heat_bands((0, cr - 8), 8, 0, True, total)
    part = jnp.sum(total, axis=0, keepdims=True)

    def pow_copy(at, j, at_slot):
        return remote(
            out_rows.at[pl.ds(pl.multiple_of(j * stride, 8), cap + 1)],
            arrived.at[pl.ds(pl.multiple_of(at_slot * stride, 8), cap + 1)],
            pow_send.at[j], pow_recv.at[at_slot], at,
        )

    def send_power(at, j):
        start = pl.multiple_of(j * stride, 8)
        fill(out_rows, start, blocks, j, power)
        out_rows[pl.ds(start + cap, 1), :] = part
        pow_copy(at, j, me).start()

    others_long(send_power)
    start = pl.multiple_of(me * stride, 8)
    fill(arrived, start, blocks, me, power)
    arrived[pl.ds(start + cap, 1), :] = part

    halo_all(0, src, "send", every)
    halo_all(1, cond, "send", every)

    def sent(at, j):
        ask_copy(at, j, j).wait_send()
        row_copy(at, j, j).wait_send()
        pow_copy(at, j, j).wait_send()

    others(sent)
    set_where.wait()
    others(lambda at, j: pow_copy(at, j, j).wait_recv())

    def add(j, total):
        return total + arrived[pl.ds(j * stride + cap, 1), :]

    sums[...] = lax.fori_loop(0, n, add, jnp.zeros((1, lanes), jnp.float32), unroll=8)

    def gather(b, carry):
        for c in range(32):
            heat[pl.ds(b * 32 + c, 1), :] = arrived[pl.ds(where_from[b, 0, c], 1), :]
        return carry

    lax.fori_loop(0, where_from.shape[0], gather, 0, unroll=4)


def thermal_kernel(
    scale, potential_in, heat, sums, inv_d, base, first_t, left_n, right_n,
    potential, temp_out, temp_new, sem,
):
    through = pltpu.make_async_copy(potential_in, potential, sem.at[0])
    through.start()
    count, lanes = heat.shape
    factor = scale / jnp.sum(sums[...])
    step, pieces = 64, 4
    chunk = count // pieces

    def put(q):
        at = pl.ds(q * chunk, chunk)
        return pltpu.make_async_copy(temp_new.at[at], temp_out.at[at], sem.at[1 + q])

    def solve(b, carry):
        at = pl.ds(pl.multiple_of(b * step, 8), step)
        warm = heat[at, :] * factor * inv_d[at, :]
        current = first_t[at, :] + warm
        for _ in range(JACOBI - 1):
            before = pltpu.roll(current, 1, 1)
            after = pltpu.roll(current, lanes - 1, 1)
            current = (base[at, :] + warm) + left_n[at, :] * before + right_n[at, :] * after
        temp_new[at, :] = current
        return carry

    for q in range(pieces):
        lax.fori_loop(q * chunk // step, (q + 1) * chunk // step, solve, 0, unroll=True)
        put(q).start()
    for q in range(pieces):
        put(q).wait()
    through.wait()


def per_device(source, sigma_ref, owner, slot, temp_old, heat_cap, conduct):
    layers, blks = lax.axis_size("layer"), lax.axis_size("blk")
    n = layers * blks
    ca, cr, lanes = source.shape
    count = temp_old.shape[0]
    cap = 2 * ca * cr // n
    stride = cap + 8
    whole, vmem = pl.BlockSpec(memory_space=pl.ANY), pl.BlockSpec(memory_space=pltpu.VMEM)

    def f32(*shape):
        return pltpu.VMEM(shape, jnp.float32)

    def i32(*shape):
        return pltpu.VMEM(shape, jnp.int32)

    field = f32(ca + 2 * WIDE, cr + 2 * ROWS, lanes)
    each = pltpu.SemaphoreType.DMA((n,))
    thermal = jax.ShapeDtypeStruct(temp_old.shape, jnp.float32)

    def exchange(*refs):
        exchange_kernel(layers, blks, *refs)

    inputs = [
        pltpu.with_memory_space_constraint(x, pltpu.HBM)
        for x in (source, sigma_ref, owner, slot, temp_old, heat_cap, conduct)
    ]
    potential = jax.ShapeDtypeStruct(source.shape, jnp.float32)
    row = jax.ShapeDtypeStruct((1, lanes), jnp.float32)
    results = pl.pallas_call(
        exchange,
        out_shape=(potential, thermal, row) + (thermal,) * 5,
        in_specs=[whole] * 7,
        out_specs=(vmem,) * 8,
        scratch_shapes=[
            f32(n * stride, lanes),
            i32(count // 32, 1, LANES), pltpu.SMEM((count // 32, 1, LANES), jnp.int32),
            i32(ca, cr), i32(ca, cr), f32(ca, cr, lanes),
            f32(count, lanes), f32(count, lanes), f32(count, lanes),
            i32(n, 1, LANES), i32(n, 1, LANES), i32(n, 1, LANES),
            i32(ca, 1, LANES), i32(n, 1, LANES),
            pltpu.SMEM((n, 1, LANES), jnp.int32),
            pltpu.SMEM((ca, 1, LANES), jnp.int32),
            pltpu.SMEM((n, 1, LANES), jnp.int32),
            f32(n * cap, lanes), f32(n * cap, lanes), f32(n * stride, lanes),
            field, field, [f32(ca + 2 * WIDE, EDGE, lanes)] * 2,
            field, field, field, field, field, field, field, field, field,
            f32(ca, cr, lanes), f32(ca * cr, lanes),
            pltpu.SemaphoreType.DMA((8,)),
            each, each, each, each, each, each,
            pltpu.SemaphoreType.DMA((2, 8)),
            pltpu.SemaphoreType.DMA((2, 8)),
        ],
        compiler_params=pltpu.CompilerParams(
            collective_id=0, has_side_effects=True, vmem_limit_bytes=40 << 20
        ),
    )(*inputs)

    def heat_step(*refs):
        thermal_kernel(float(source.size * n), *refs)

    return pl.pallas_call(
        heat_step,
        out_shape=(potential, thermal),
        in_specs=[whole] + [vmem] * 7,
        out_specs=(whole,) * 2,
        scratch_shapes=[f32(count, lanes), pltpu.SemaphoreType.DMA((5,))],
        compiler_params=pltpu.CompilerParams(vmem_limit_bytes=24 << 20),
    )(*results)


def solution(mesh):
    field = P("layer", "blk", None)
    index = P("layer", "blk")
    thermal = P(("blk", "layer"), None)
    return jax.shard_map(
        per_device,
        mesh=mesh,
        in_specs=(field, field, index, index, thermal, thermal, thermal),
        out_specs=(field, thermal),
        check_vma=False,
    )
```
